512 devices in a mesh: hx: 32 (over x, z), hy: 16 (over y, core).
Axes of the slice: x: 4, y: 8, z: 8, core: 2. Of those that a mesh axis runs over, the one named last changes fastest.
Arguments:
- source: float32 [2048, 2048], P('hx', 'hy'), may hold values from -27 to 27
- coeffs: float32 [65, 65], replicated, may hold values from -0.13 to 0.13
- row_factor: float32 [2048, 2048], P('hx'), may hold values from -0.075 to 0.575
- col_factor: float32 [2048, 2048], P(None, 'hy'), may hold values from -0.075 to 0.575
- tile_mask: int32 [8, 8], replicated, may hold values 0 or 1
Outputs:
- solution: float32 [2048, 2048], P('hx', 'hy')
- norm_values: float32 [8], replicated
The draws below stay inside these ranges and needn't reach their ends.
Inputs may be any that keep to these rules, and one draw needn't show every extreme that they name: tile_mask[a, b] is 1 where the tile of rows a * 256 onward and columns b * 256 onward carries a block coupling, else 0.
All inputs are finite; a program needn't handle non-finite values.
Results may differ from the reference program's by a relative error of at most 0.0003.
Values sent between devices are 32-bit elements; how exact they have to be, the bound alone decides.
A program may use at most 64 MiB of HBM per device.

```python
import math
import jax
import jax.numpy as jnp
from jax import lax

TILE = 256
BAND = 32
ITERS = 8
NX = 2048
NY = 2048


def draw_source(key, part):
    noise_key = jax.random.fold_in(jax.random.fold_in(key, 101), 0)
    col_key = jax.random.fold_in(jax.random.fold_in(key, 101), 2)
    row_place = jnp.arange(NX, dtype=jnp.float32) / NX
    col_level = 10.0 ** jax.random.uniform(col_key, (NY,), jnp.float32)
    noise = jax.random.truncated_normal(noise_key, -4.0, 4.0, (NX, NY), jnp.float32)
    row_level = 10.0 ** row_place
    return noise * row_level[:, None] * col_level[None, :] / 15.0


def draw_coeffs(key, part):
    tap_count = 2 * BAND + 1
    noise_key = jax.random.fold_in(key, 202)
    offsets = jnp.abs(jnp.arange(tap_count, dtype=jnp.float32) - BAND)
    decay = 0.03 / jnp.sqrt((1.0 + offsets)[:, None] * (1.0 + offsets)[None, :])
    noise = jax.random.truncated_normal(noise_key, -4.0, 4.0, (tap_count, tap_count), jnp.float32)
    return noise * decay


def diagonal_part():
    same_place = jnp.arange(NX)[:, None] % TILE == jnp.arange(NY)[None, :] % TILE
    return 0.5 * same_place.astype(jnp.float32)


def draw_row_factor(key, part):
    noise_key = jax.random.fold_in(key, 303)
    noise = jax.random.truncated_normal(noise_key, -4.0, 4.0, (NX, NY), jnp.float32)
    return diagonal_part() + 0.3 * noise / math.sqrt(TILE)


def draw_col_factor(key, part):
    noise_key = jax.random.fold_in(key, 404)
    noise = jax.random.truncated_normal(noise_key, -4.0, 4.0, (NX, NY), jnp.float32)
    return diagonal_part() + 0.3 * noise / math.sqrt(TILE)


def plant(values, key, least, largest):
    dims = values.shape
    index_at = [jax.random.randint(jax.random.fold_in(key, axis), (), 0, dims[axis]) for axis in range(len(dims))]
    values = values.at[tuple(index_at)].set(least)
    longest = dims.index(max(dims))
    index_at[longest] = (index_at[longest] + 1) % dims[longest]
    return values.at[tuple(index_at)].set(largest)


def setup_inputs(seed: int = 0) -> dict:
    key_of = jax.random.split(jax.random.key(seed), 6)
    return {
        "source": draw_source(jax.random.fold_in(key_of[5], 71), 0),
        "coeffs": draw_coeffs(jax.random.fold_in(key_of[5], 71), 0),
        "row_factor": draw_row_factor(jax.random.fold_in(key_of[5], 71), 0),
        "col_factor": draw_col_factor(jax.random.fold_in(key_of[5], 71), 0),
        "tile_mask": plant((jax.random.randint(key_of[4], (NX // TILE, NY // TILE), 0, 2) < 1).astype(jnp.int32), jax.random.fold_in(key_of[4], 1), 0, 1),
    }


relax_step = 0.25
highest = lax.Precision.HIGHEST
tiny_square = 1e-06

def banded_product(field_now, coeffs):
    band_width = (coeffs.shape[0] - 1) // 2
    row_count, col_count = field_now.shape
    full_shape = (row_count + 2 * band_width, col_count + 2 * band_width)
    spectrum = jnp.fft.rfft2(field_now, s=full_shape) * jnp.fft.rfft2(coeffs, s=full_shape)
    full_conv = jnp.fft.irfft2(spectrum, s=full_shape)
    return full_conv[band_width:band_width + row_count, band_width:band_width + col_count]

def tile_term(field_now, row_factor, col_factor, tile_mask):
    tiles_down, tiles_across = tile_mask.shape
    shape_four = (tiles_down, TILE, tiles_across, TILE)
    mixed = jnp.einsum('aibj,ajbl->aibl', row_factor.reshape(shape_four), field_now.reshape(shape_four), precision=highest)
    result = jnp.einsum('aibk,akbl->aibl', mixed, col_factor.reshape(shape_four), precision=highest)
    weights = tile_mask.astype(jnp.float32)[:, None, :, None]
    return (result * weights).reshape(field_now.shape)

def reference(source, coeffs, row_factor, col_factor, tile_mask):
    solution = source
    squares = []
    for step_index in range(ITERS):
        applied = solution + banded_product(solution, coeffs) + tile_term(solution, row_factor, col_factor, tile_mask)
        residual = source - applied
        squares.append(jnp.sum(residual * residual))
        solution = solution + relax_step * residual
    norm_values = jnp.sqrt(jnp.stack(squares) / (NX * NY) + tiny_square)
    return (solution, norm_values)
```

```python
import functools

import jax
import jax.numpy as jnp
import ml_dtypes
import numpy as np
from jax import lax
from jax.experimental import pallas as pl
from jax.experimental.pallas import tpu as pltpu
from jax.sharding import PartitionSpec as P

TILE = 256
BAND = 32
ITERS = 8
ROWS = 64
COLS = 128
GROUP = TILE // ROWS
LONG_ROWS = ROWS + 2 * BAND
LONG_COLS = COLS + 2 * BAND
HALF = LONG_COLS // 2 + 1
Z_SIZE = 8
STEP = 0.25
TINY = 1e-06
MESH = pl.DeviceIdType.MESH
F32 = jnp.float32
BF16 = jnp.bfloat16


def split_table(table):
    high = table.astype(np.float32).astype(ml_dtypes.bfloat16)
    low = (table - high.astype(np.float64)).astype(np.float32).astype(ml_dtypes.bfloat16)
    return np.concatenate([high, low], axis=0)


def tables():
    lane = np.arange(COLS)
    freq_col = np.arange(COLS)
    kept = (freq_col < HALF).astype(np.float64)
    place = np.concatenate([lane + BAND, np.where(lane < BAND, lane + BAND + COLS, lane - (COLS - BAND))])
    used = np.concatenate([np.ones(COLS), ((lane < BAND) | (lane >= COLS - BAND)).astype(np.float64)])
    angle = 2 * np.pi * ((place[:, None] * freq_col[None, :]) % LONG_COLS) / LONG_COLS
    weight = used[:, None] * kept[None, :]
    col_forward = np.concatenate([np.cos(angle) * weight, -np.sin(angle) * weight], axis=1)
    tap = np.arange(LONG_ROWS)
    angle = 2 * np.pi * ((tap[:, None] * freq_col[None, :]) % LONG_COLS) / LONG_COLS
    weight = (tap <= 2 * BAND)[:, None] * kept[None, :]
    coeff_forward = np.concatenate([np.cos(angle) * weight, -np.sin(angle) * weight], axis=1)
    row = np.arange(LONG_ROWS)
    angle = 2 * np.pi * ((row[:, None] * row[None, :]) % LONG_ROWS) / LONG_ROWS
    row_forward = np.concatenate([np.cos(angle), np.sin(angle)], axis=0)
    target = np.arange(ROWS) + 2 * BAND
    angle = 2 * np.pi * ((target[:, None] * row[None, :]) % LONG_ROWS) / LONG_ROWS
    row_inverse = np.concatenate([np.cos(angle), np.sin(angle)], axis=0)
    target = lane + 2 * BAND
    angle = 2 * np.pi * ((freq_col[:, None] * target[None, :]) % LONG_COLS) / LONG_COLS
    scale = np.where((freq_col == 0) | (freq_col == HALF - 1), 1.0, 2.0) * kept / (LONG_ROWS * LONG_COLS)
    col_inverse = np.concatenate([np.cos(angle) * scale[:, None], -np.sin(angle) * scale[:, None]], axis=0)
    return [split_table(t) for t in (col_forward, coeff_forward, row_forward, row_inverse, col_inverse)]


def split(value):
    high = value.astype(BF16)
    return high, (value - high.astype(F32)).astype(BF16)


def dot(a, b):
    return jnp.dot(a, b, preferred_element_type=F32)


def dot_split(a, b):
    (a_high, a_low), (b_high, b_low) = a, b
    return dot(a_high, b_high) + dot(a_high, b_low) + dot(a_low, b_high)


def parts(ref):
    half = ref.shape[0] // 2
    return ref[0:half, :], ref[half:, :]


def kernel(
    sizes,
    source_hbm, coeffs_hbm, row_hbm, col_hbm, mask_ref,
    col_forward_hbm, coeff_forward_hbm, row_forward_hbm, row_inverse_hbm, col_inverse_hbm,
    out_ref, norm_ref,
    field, strips, packed, mixed_send, mixed_recv, accum, squares,
    coeffs_raw, coeffs_pad, row_tile, col_tile, row_parts, col_parts, coeff_re, coeff_im,
    col_forward, coeff_forward, row_forward, row_inverse, col_inverse,
    sum_y, sum_z, sum_x,
    local_sem, tile_send, tile_recv, edge_send, edge_recv, strip_send, strip_recv,
    mixed_send_sem, mixed_recv_sem, sum_send, sum_y_recv, sum_z_recv, sum_x_recv,
):
    n_hx, n_hy, n_z = sizes
    n_x = n_hx // n_z
    hx, hy = lax.axis_index("hx"), lax.axis_index("hy")
    place = lax.rem(hx, GROUP)
    first = hx - place
    tile_row, tile_col = hx // GROUP, hy // 2
    core = lax.rem(hy, 2)
    x, z = hx // n_z, lax.rem(hx, n_z)
    up, down, left, right = hx > 0, hx < n_hx - 1, hy > 0, hy < n_hy - 1
    own_rows = pl.ds(pl.multiple_of(BAND + place * ROWS, BAND), ROWS)

    for slot in range(2):
        field[slot, 0:BAND, :] = jnp.zeros((BAND, COLS), F32)
        field[slot, BAND + TILE :, :] = jnp.zeros((BAND, COLS), F32)
        for side in range(2):
            strips[slot, side] = jnp.zeros((4 * 8, COLS), F32)
    coeffs_pad[...] = jnp.zeros_like(coeffs_pad)

    local = [
        pltpu.make_async_copy(source_hbm, field.at[0, own_rows, :], local_sem.at[0]),
        pltpu.make_async_copy(coeffs_hbm, coeffs_raw, local_sem.at[1]),
        pltpu.make_async_copy(
            row_hbm.at[:, pl.ds(pl.multiple_of(tile_col * TILE, TILE), TILE)], row_tile, local_sem.at[2]
        ),
        pltpu.make_async_copy(
            col_hbm.at[pl.ds(pl.multiple_of(tile_row * TILE, TILE), TILE), :], col_tile, local_sem.at[3]
        ),
        pltpu.make_async_copy(col_forward_hbm, col_forward, local_sem.at[4]),
        pltpu.make_async_copy(coeff_forward_hbm, coeff_forward, local_sem.at[5]),
        pltpu.make_async_copy(row_forward_hbm, row_forward, local_sem.at[6]),
        pltpu.make_async_copy(row_inverse_hbm, row_inverse, local_sem.at[7]),
        pltpu.make_async_copy(col_inverse_hbm, col_inverse, local_sem.at[8]),
    ]
    for item in local:
        item.start()

    barrier = pltpu.get_barrier_semaphore()

    def greet(to_hx, to_hy):
        pl.semaphore_signal(barrier, inc=1, device_id=(to_hx, to_hy), device_id_type=MESH)

    def greet_y(i, carry):
        greet(hx, lax.rem(hy + i, n_hy))
        return carry

    def greet_z(i, carry):
        greet(x * n_z + lax.rem(z + i, n_z), hy)
        return carry

    def greet_x(i, carry):
        greet(lax.rem(x + i, n_x) * n_z + z, hy)
        return carry

    lax.fori_loop(1, n_hy, greet_y, 0)
    lax.fori_loop(1, n_z, greet_z, 0)
    lax.fori_loop(1, n_x, greet_x, 0)
    for there, to_hx in ((up, hx - 1), (down, hx + 1)):
        @pl.when(there)
        def _():
            greet(to_hx, hy)

            @pl.when(left)
            def _():
                greet(to_hx, hy - 1)

            @pl.when(right)
            def _():
                greet(to_hx, hy + 1)

    lane_group = lax.broadcasted_iota(jnp.int32, (8, COLS), 1) // BAND

    def pack(value):
        for half in range(2):
            to_left = to_right = None
            for g in range(4):
                start = half * BAND + 8 * g
                rolled = value[start : start + 8, :]
                if g:
                    rolled = pltpu.roll(rolled, BAND * g, axis=1)
                if to_left is None:
                    to_left = to_right = rolled
                else:
                    to_left = jnp.where(lane_group == g, rolled, to_left)
                    to_right = jnp.where(lane_group == (g + 3) % 4, rolled, to_right)
            packed[0, 8 * half : 8 * half + 8, :] = to_left
            packed[1, 8 * half : 8 * half + 8, :] = to_right

    local[0].wait()
    source = field[0, own_rows, :]
    accum[...] = source
    pack(source)

    local[2].wait()
    local[3].wait()
    active = mask_ref[tile_row, tile_col].astype(F32)
    high, low = split(row_tile[...] * active)
    row_parts[0:ROWS, :] = high
    row_parts[ROWS:, :] = low
    for which, start in enumerate((core, 1 - core)):
        high, low = split(col_tile[pl.ds(pl.multiple_of(start * COLS, COLS), COLS), :])
        col_parts[which, 0:COLS, :] = high
        col_parts[which, COLS:, :] = low
    local[1].wait()
    coeffs_pad[0 : 2 * BAND + 1, 0 : 2 * BAND + 1] = coeffs_raw[...]
    local[5].wait()
    local[6].wait()
    by_col = dot_split(split(coeffs_pad[...]), parts(coeff_forward))
    turned = dot_split(parts(row_forward), split(by_col))
    coeff_re[...] = turned[0:LONG_ROWS, 0:COLS] + turned[LONG_ROWS:, COLS:]
    coeff_im[...] = turned[0:LONG_ROWS, COLS:] - turned[LONG_ROWS:, 0:COLS]
    for i in (4, 7, 8):
        local[i].wait()

    count = (up.astype(jnp.int32) + down.astype(jnp.int32)) * (
        1 + left.astype(jnp.int32) + right.astype(jnp.int32)
    ) + (n_hy - 1 + n_z - 1 + n_x - 1)
    pl.semaphore_wait(barrier, count)

    def remote(source_ref, target_ref, send_sem, recv_sem, to_hx, to_hy):
        return pltpu.make_async_remote_copy(
            src_ref=source_ref, dst_ref=target_ref, send_sem=send_sem, recv_sem=recv_sem,
            device_id=(to_hx, to_hy), device_id_type=MESH,
        )

    def tile_copy(slot, which):
        block = field.at[slot, own_rows, :]
        return remote(block, block, tile_send.at[which], tile_recv.at[slot, place], first + which, hy)

    def tile_arrival(slot, which):
        block = field.at[slot, BAND + which * ROWS : BAND + (which + 1) * ROWS, :]
        return remote(block, block, tile_send.at[which], tile_recv.at[slot, which], first + which, hy)

    def edge_up(slot):
        return remote(
            field.at[slot, BAND : 2 * BAND, :], field.at[slot, BAND + TILE : 2 * BAND + TILE, :],
            edge_send.at[0], edge_recv.at[slot, 1], hx - 1, hy,
        )

    def edge_down(slot):
        return remote(
            field.at[slot, TILE : TILE + BAND, :], field.at[slot, 0:BAND, :],
            edge_send.at[1], edge_recv.at[slot, 0], hx + 1, hy,
        )

    def edge_arrival(slot, which):
        rows = field.at[slot, 0:BAND, :] if which == 0 else field.at[slot, BAND + TILE : 2 * BAND + TILE, :]
        return remote(rows, rows, edge_send.at[which], edge_recv.at[slot, which], hx, hy)

    def strip_copy(slot, side, which):
        to_hy = hy - 1 if side == 0 else hy + 1
        if which == 0:
            rows, target, sem, to_hx = packed.at[side, 0:8, :], strips.at[slot, 1 - side, 24:32, :], 2, hx - 1
        elif which == 1:
            rows, target, sem, to_hx = packed.at[side], strips.at[slot, 1 - side, 8:24, :], 1, hx
        else:
            rows, target, sem, to_hx = packed.at[side, 8:16, :], strips.at[slot, 1 - side, 0:8, :], 0, hx + 1
        return remote(rows, target, strip_send.at[side, which], strip_recv.at[slot, 1 - side, sem], to_hx, to_hy)

    def strip_arrival(slot, side, which):
        start, stop = ((0, 8), (8, 24), (24, 32))[which]
        rows = strips.at[slot, side, start:stop, :]
        return remote(rows, rows, strip_send.at[side, which], strip_recv.at[slot, side, which], hx, hy)

    def mixed_copy(slot):
        return remote(
            mixed_send, mixed_recv.at[slot], mixed_send_sem, mixed_recv_sem.at[slot], hx, hy + 1 - 2 * core
        )

    def on(conditions, action):
        if conditions:
            pl.when(functools.reduce(jnp.logical_and, conditions))(action)
        else:
            action()

    row_there = ((0, (up,)), (1, ()), (2, (down,)))
    side_there = ((0, left), (1, right))

    def all_sends(slot, act):
        for distance in (3, 2, 1):
            for step in (-distance, distance):
                which = place + step
                on([which >= 0, which < GROUP], lambda which=which: act(tile_copy(slot, which)))
        on([place == 0, up], lambda: act(edge_up(slot)))
        on([place == GROUP - 1, down], lambda: act(edge_down(slot)))
        for side, beside in side_there:
            for which, there in row_there:
                on([beside, *there], lambda side=side, which=which: act(strip_copy(slot, side, which)))

    def iteration(k, carry):
        slot = lax.rem(k, 2)
        all_sends(slot, lambda item: item.start())

        on([place == 0, up], lambda: edge_arrival(slot, 0).wait_recv())
        on([place == GROUP - 1, down], lambda: edge_arrival(slot, 1).wait_recv())
        for which in range(GROUP):
            near = [jnp.abs(place - which) == 1]
            on(near, lambda which=which: tile_arrival(slot, which).wait_recv())
        for side, beside in side_there:
            for which, there in row_there:
                on([beside, *there], lambda side=side, which=which: strip_arrival(slot, side, which).wait_recv())

        tall = field[slot, pl.ds(pl.multiple_of(place * ROWS, ROWS), LONG_ROWS), :]
        from_left, from_right = strips[slot, 0], strips[slot, 1]
        pieces = []
        for t in range(4):
            piece_left, piece_right = from_left[8 * t : 8 * t + 8, :], from_right[8 * t : 8 * t + 8, :]
            for g in range(4):
                piece = jnp.where(
                    lane_group == g, piece_right, jnp.where(lane_group == (g + 3) % 4, piece_left, 0.0)
                )
                pieces.append(pltpu.roll(piece, COLS - BAND * g, axis=1) if g else piece)
        wide = jnp.concatenate([tall, jnp.concatenate(pieces, axis=0)], axis=1)
        by_col = dot_split(split(wide), parts(col_forward))
        turned = dot_split(parts(row_forward), split(by_col))
        freq_re = turned[0:LONG_ROWS, 0:COLS] + turned[LONG_ROWS:, COLS:]
        freq_im = turned[0:LONG_ROWS, COLS:] - turned[LONG_ROWS:, 0:COLS]
        c_re, c_im = coeff_re[...], coeff_im[...]
        product = jnp.concatenate([freq_re * c_re - freq_im * c_im, freq_re * c_im + freq_im * c_re], axis=1)
        turned = dot_split(parts(row_inverse), split(product))
        back = jnp.concatenate(
            [turned[0:ROWS, 0:COLS] - turned[ROWS:, COLS:], turned[0:ROWS, COLS:] + turned[ROWS:, 0:COLS]], axis=1
        )
        band = dot_split(split(back), parts(col_inverse))

        for which in range(GROUP):
            far = [jnp.abs(place - which) > 1]
            on(far, lambda which=which: tile_arrival(slot, which).wait_recv())
        mixed = dot_split(parts(row_parts), split(field[slot, BAND : BAND + TILE, :]))
        mixed_send[...] = mixed
        mixed_copy(slot).start()
        total = band + dot_split(split(mixed), parts(col_parts.at[0]))
        mixed_copy(slot).wait_recv()
        total = total + dot_split(split(mixed_recv[slot]), parts(col_parts.at[1]))

        keep = jnp.where(k == 0, 0.0, 1.0 - STEP)
        take = jnp.where(k == 0, 1.0, STEP)
        residual = keep * field[slot, own_rows, :] - take * total
        all_sends(slot, lambda item: item.wait_send())
        mixed_copy(slot).wait_send()
        field[1 - slot, own_rows, :] = residual
        pack(residual)
        accum[...] += STEP * residual
        squares[pl.ds(k, 1), :] = jnp.sum(residual * residual, axis=0, keepdims=True)
        return carry

    lax.fori_loop(0, ITERS, iteration, 0)
    out_ref[...] = accum[...]

    def gather(total, held, recv_sem, index, size, device):
        held[index] = total

        def copy(to, at):
            return remote(
                held.at[index], held.at[at], sum_send.at[to], recv_sem.at[at], *device(to)
            )

        def start(i, carry):
            copy(lax.rem(index + i, size), index).start()
            return carry

        def wait(i, carry):
            other = lax.rem(index + i, size)
            item = remote(held.at[other], held.at[other], sum_send.at[other], recv_sem.at[other], *device(other))
            item.wait_recv()
            copy(other, index).wait_send()
            return carry

        lax.fori_loop(1, size, start, 0)
        lax.fori_loop(1, size, wait, 0)
        return jnp.sum(held[...], axis=0)

    total = gather(squares[...], sum_y, sum_y_recv, hy, n_hy, lambda to: (hx, to))
    total = gather(total, sum_z, sum_z_recv, z, n_z, lambda to: (x * n_z + to, hy))
    if n_x > 1:
        total = gather(total, sum_x, sum_x_recv, x, n_x, lambda to: (to * n_z + z, hy))
    mean = jnp.sum(total, axis=1, keepdims=True) / (ROWS * COLS * n_hx * n_hy)
    norm_ref[...] = jnp.broadcast_to(jnp.sqrt(mean + TINY), norm_ref.shape)


def local_step(sizes, source, coeffs, row_factor, col_factor, tile_mask):
    n_hx, n_hy, n_z = sizes
    constants = [jnp.asarray(t) for t in tables()]
    any_spec = pl.BlockSpec(memory_space=pl.ANY)
    vmem_spec = pl.BlockSpec(memory_space=pltpu.VMEM)
    dma = pltpu.SemaphoreType.DMA
    taps = 2 * BAND + 1
    scratch = [
        pltpu.VMEM((2, TILE + 2 * BAND, COLS), F32),
        pltpu.VMEM((2, 2, 32, COLS), F32),
        pltpu.VMEM((2, 16, COLS), F32),
        pltpu.VMEM((ROWS, COLS), F32),
        pltpu.VMEM((2, ROWS, COLS), F32),
        pltpu.VMEM((ROWS, COLS), F32),
        pltpu.VMEM((ITERS, COLS), F32),
        pltpu.VMEM((taps, taps), F32),
        pltpu.VMEM((LONG_ROWS, COLS), F32),
        pltpu.VMEM((ROWS, TILE), F32),
        pltpu.VMEM((TILE, COLS), F32),
        pltpu.VMEM((2 * ROWS, TILE), BF16),
        pltpu.VMEM((2, 2 * COLS, COLS), BF16),
        pltpu.VMEM((LONG_ROWS, COLS), F32),
        pltpu.VMEM((LONG_ROWS, COLS), F32),
        *[pltpu.VMEM(c.shape, c.dtype) for c in constants],
        pltpu.VMEM((n_hy, ITERS, COLS), F32),
        pltpu.VMEM((n_z, ITERS, COLS), F32),
        pltpu.VMEM((n_hx // n_z, ITERS, COLS), F32),
        dma((9,)),
        dma((GROUP,)), dma((2, GROUP)),
        dma((2,)), dma((2, 2)),
        dma((2, 3)), dma((2, 2, 3)),
        dma, dma((2,)),
        dma((max(n_hy, n_z),)), dma((n_hy,)), dma((n_z,)), dma((n_hx // n_z,)),
    ]
    result, norms = pl.pallas_call(
        functools.partial(kernel, sizes),
        out_shape=(jax.ShapeDtypeStruct((ROWS, COLS), F32), jax.ShapeDtypeStruct((ITERS, COLS), F32)),
        in_specs=[any_spec] * 4 + [pl.BlockSpec(memory_space=pltpu.SMEM)] + [any_spec] * 5,
        out_specs=(vmem_spec, vmem_spec),
        scratch_shapes=scratch,
        compiler_params=pltpu.CompilerParams(collective_id=0, has_side_effects=True),
        name="richardson",
    )(source, coeffs, row_factor, col_factor, tile_mask, *constants)
    return result, norms[:, 0]


def solution(mesh):
    n_hx, n_hy = mesh.shape["hx"], mesh.shape["hy"]
    sizes = (n_hx, n_hy, min(n_hx, Z_SIZE))
    in_specs = (P("hx", "hy"), P(), P("hx", None), P(None, "hy"), P())
    out_specs = (P("hx", "hy"), P())
    return jax.shard_map(
        functools.partial(local_step, sizes), mesh=mesh, in_specs=in_specs, out_specs=out_specs, check_vma=False
    )
```

```python
import functools

import jax
import jax.numpy as jnp
import ml_dtypes
import numpy as np
from jax import lax
from jax.experimental import pallas as pl
from jax.experimental.pallas import tpu as pltpu
from jax.sharding import PartitionSpec as P

TILE = 256
BAND = 32
ITERS = 8
ROWS = 64
COLS = 128
GROUP = TILE // ROWS
LONG_ROWS = ROWS + 2 * BAND
LONG_COLS = COLS + 2 * BAND
HALF = LONG_COLS // 2 + 1
Z_SIZE = 8
NEAR = 1
STEP = 0.25
TINY = 1e-06
MESH = pl.DeviceIdType.MESH
F32 = jnp.float32
BF16 = jnp.bfloat16


def split_table(table):
    high = table.astype(np.float32).astype(ml_dtypes.bfloat16)
    low = (table - high.astype(np.float64)).astype(np.float32).astype(ml_dtypes.bfloat16)
    return np.concatenate([high, low], axis=0)


def tables():
    lane = np.arange(COLS)
    freq_col = np.arange(COLS)
    kept = (freq_col < HALF).astype(np.float64)
    place = np.concatenate([lane + BAND, np.where(lane < BAND, lane + BAND + COLS, lane - (COLS - BAND))])
    used = np.concatenate([np.ones(COLS), ((lane < BAND) | (lane >= COLS - BAND)).astype(np.float64)])
    angle = 2 * np.pi * ((place[:, None] * freq_col[None, :]) % LONG_COLS) / LONG_COLS
    weight = used[:, None] * kept[None, :]
    col_forward = np.concatenate([np.cos(angle) * weight, -np.sin(angle) * weight], axis=1)
    tap = np.arange(LONG_ROWS)
    angle = 2 * np.pi * ((tap[:, None] * freq_col[None, :]) % LONG_COLS) / LONG_COLS
    weight = (tap <= 2 * BAND)[:, None] * kept[None, :]
    coeff_forward = np.concatenate([np.cos(angle) * weight, -np.sin(angle) * weight], axis=1)
    row = np.arange(LONG_ROWS)
    angle = 2 * np.pi * ((row[:, None] * row[None, :]) % LONG_ROWS) / LONG_ROWS
    row_forward = np.concatenate([np.cos(angle), np.sin(angle)], axis=0)
    target = np.arange(ROWS) + 2 * BAND
    angle = 2 * np.pi * ((target[:, None] * row[None, :]) % LONG_ROWS) / LONG_ROWS
    row_inverse = np.concatenate([np.cos(angle), np.sin(angle)], axis=0)
    target = lane + 2 * BAND
    angle = 2 * np.pi * ((freq_col[:, None] * target[None, :]) % LONG_COLS) / LONG_COLS
    scale = np.where((freq_col == 0) | (freq_col == HALF - 1), 1.0, 2.0) * kept / (LONG_ROWS * LONG_COLS)
    col_inverse = np.concatenate([np.cos(angle) * scale[:, None], -np.sin(angle) * scale[:, None]], axis=0)
    return [split_table(t) for t in (col_forward, coeff_forward, row_forward, row_inverse, col_inverse)]


def split(value):
    high = value.astype(BF16)
    return high, (value - high.astype(F32)).astype(BF16)


def dot(a, b):
    return jnp.dot(a, b, preferred_element_type=F32)


def dot_split(a, b):
    (a_high, a_low), (b_high, b_low) = a, b
    return dot(a_high, b_high) + dot(a_high, b_low) + dot(a_low, b_high)


def parts(ref):
    half = ref.shape[0] // 2
    return ref[0:half, :], ref[half:, :]


def kernel(
    sizes,
    source_hbm, coeffs_hbm, row_hbm, col_hbm, mask_ref,
    col_forward_hbm, coeff_forward_hbm, row_forward_hbm, row_inverse_hbm, col_inverse_hbm,
    out_ref, norm_ref,
    field, products, partner, strips, packed, mixed_send, mixed_recv, accum, squares,
    coeffs_raw, coeffs_pad, row_tile, col_tile, row_near, row_far, col_parts, coeff_re, coeff_im,
    col_forward, coeff_forward, row_forward, row_inverse, col_inverse,
    sum_y, sum_z, sum_x,
    local_sem, tile_send, tile_recv, partner_send, partner_recv, edge_send, edge_recv, strip_send, strip_recv,
    mixed_send_sem, mixed_recv_sem, sum_send, sum_y_recv, sum_z_recv, sum_x_recv,
):
    n_hx, n_hy, n_z = sizes
    n_x = n_hx // n_z
    hx, hy = lax.axis_index("hx"), lax.axis_index("hy")
    place = lax.rem(hx, GROUP)
    first = hx - place
    tile_row, tile_col = hx // GROUP, hy // 2
    core = lax.rem(hy, 2)
    x, z = hx // n_z, lax.rem(hx, n_z)
    up, down, left, right = hx > 0, hx < n_hx - 1, hy > 0, hy < n_hy - 1
    own_rows = pl.ds(pl.multiple_of(BAND + place * ROWS, BAND), ROWS)
    own_product = pl.ds(pl.multiple_of(place * ROWS, ROWS), ROWS)
    beside_core = hy + 1 - 2 * core

    for slot in range(2):
        field[slot] = jnp.zeros(field.shape[1:], F32)
        products[slot] = jnp.zeros(products.shape[1:], F32)
        for side in range(2):
            strips[slot, side] = jnp.zeros((4 * 8, COLS), F32)
    coeffs_pad[...] = jnp.zeros_like(coeffs_pad)

    local = [
        pltpu.make_async_copy(source_hbm, field.at[0, own_rows, :], local_sem.at[0]),
        pltpu.make_async_copy(coeffs_hbm, coeffs_raw, local_sem.at[1]),
        pltpu.make_async_copy(
            row_hbm.at[:, pl.ds(pl.multiple_of(tile_col * TILE, TILE), TILE)], row_tile, local_sem.at[2]
        ),
        pltpu.make_async_copy(
            col_hbm.at[pl.ds(pl.multiple_of(tile_row * TILE, TILE), TILE), :], col_tile, local_sem.at[3]
        ),
        pltpu.make_async_copy(col_forward_hbm, col_forward, local_sem.at[4]),
        pltpu.make_async_copy(coeff_forward_hbm, coeff_forward, local_sem.at[5]),
        pltpu.make_async_copy(row_forward_hbm, row_forward, local_sem.at[6]),
        pltpu.make_async_copy(row_inverse_hbm, row_inverse, local_sem.at[7]),
        pltpu.make_async_copy(col_inverse_hbm, col_inverse, local_sem.at[8]),
    ]
    for item in local:
        item.start()

    barrier = pltpu.get_barrier_semaphore()

    def greet(to_hx, to_hy):
        pl.semaphore_signal(barrier, inc=1, device_id=(to_hx, to_hy), device_id_type=MESH)

    def greet_y(i, carry):
        greet(hx, lax.rem(hy + i, n_hy))
        return carry

    def greet_z(i, carry):
        greet(x * n_z + lax.rem(z + i, n_z), hy)
        return carry

    def greet_x(i, carry):
        greet(lax.rem(x + i, n_x) * n_z + z, hy)
        return carry

    lax.fori_loop(1, n_hy, greet_y, 0)
    lax.fori_loop(1, n_z, greet_z, 0)
    lax.fori_loop(1, n_x, greet_x, 0)
    for there, to_hx in ((up, hx - 1), (down, hx + 1)):
        @pl.when(there)
        def _():
            greet(to_hx, hy)

            @pl.when(left)
            def _():
                greet(to_hx, hy - 1)

            @pl.when(right)
            def _():
                greet(to_hx, hy + 1)

    lane_group = lax.broadcasted_iota(jnp.int32, (8, COLS), 1) // BAND

    def pack(value):
        for half in range(2):
            to_left = to_right = None
            for g in range(4):
                start = half * BAND + 8 * g
                rolled = value[start : start + 8, :]
                if g:
                    rolled = pltpu.roll(rolled, BAND * g, axis=1)
                if to_left is None:
                    to_left = to_right = rolled
                else:
                    to_left = jnp.where(lane_group == g, rolled, to_left)
                    to_right = jnp.where(lane_group == (g + 3) % 4, rolled, to_right)
            packed[0, 8 * half : 8 * half + 8, :] = to_left
            packed[1, 8 * half : 8 * half + 8, :] = to_right

    local[0].wait()
    source = field[0, own_rows, :]
    accum[...] = source
    pack(source)

    local[2].wait()
    local[3].wait()
    active = mask_ref[tile_row, tile_col].astype(F32)
    distance = jnp.abs(lax.broadcasted_iota(jnp.int32, (ROWS, TILE), 1) // ROWS - place)
    is_near = (distance >= 1) & (distance <= NEAR)
    for parts_of, chosen in ((row_near, is_near), (row_far, ~is_near)):
        high, low = split(jnp.where(chosen, row_tile[...] * active, 0.0))
        parts_of[0:ROWS, :] = high
        parts_of[ROWS:, :] = low
    for which, start in enumerate((core, 1 - core)):
        high, low = split(col_tile[pl.ds(pl.multiple_of(start * COLS, COLS), COLS), :])
        col_parts[which, 0:COLS, :] = high
        col_parts[which, COLS:, :] = low
    local[1].wait()
    coeffs_pad[0 : 2 * BAND + 1, 0 : 2 * BAND + 1] = coeffs_raw[...]
    local[5].wait()
    local[6].wait()
    by_col = dot_split(split(coeffs_pad[...]), parts(coeff_forward))
    turned = dot_split(parts(row_forward), split(by_col))
    coeff_re[...] = turned[0:LONG_ROWS, 0:COLS] + turned[LONG_ROWS:, COLS:]
    coeff_im[...] = turned[0:LONG_ROWS, COLS:] - turned[LONG_ROWS:, 0:COLS]
    for i in (4, 7, 8):
        local[i].wait()

    count = (up.astype(jnp.int32) + down.astype(jnp.int32)) * (
        1 + left.astype(jnp.int32) + right.astype(jnp.int32)
    ) + (n_hy - 1 + n_z - 1 + n_x - 1)
    pl.semaphore_wait(barrier, count)

    def remote(source_ref, target_ref, send_sem, recv_sem, to_hx, to_hy):
        return pltpu.make_async_remote_copy(
            src_ref=source_ref, dst_ref=target_ref, send_sem=send_sem, recv_sem=recv_sem,
            device_id=(to_hx, to_hy), device_id_type=MESH,
        )

    def tile_copy(slot, which, near):
        block = field.at[slot, own_rows, :] if near else products.at[slot, own_product, :]
        return remote(block, block, tile_send.at[which], tile_recv.at[slot, place], first + which, hy)

    def tile_arrival(slot, which, near):
        block = field.at[slot, BAND + which * ROWS : BAND + (which + 1) * ROWS, :]
        if not near:
            block = products.at[slot, which * ROWS : (which + 1) * ROWS, :]
        return remote(block, block, tile_send.at[which], tile_recv.at[slot, which], first + which, hy)

    def edge_up(slot):
        return remote(
            field.at[slot, BAND : 2 * BAND, :], field.at[slot, BAND + TILE : 2 * BAND + TILE, :],
            edge_send.at[0], edge_recv.at[slot, 1], hx - 1, hy,
        )

    def edge_down(slot):
        return remote(
            field.at[slot, TILE : TILE + BAND, :], field.at[slot, 0:BAND, :],
            edge_send.at[1], edge_recv.at[slot, 0], hx + 1, hy,
        )

    def edge_arrival(slot, which):
        rows = field.at[slot, 0:BAND, :] if which == 0 else field.at[slot, BAND + TILE : 2 * BAND + TILE, :]
        return remote(rows, rows, edge_send.at[which], edge_recv.at[slot, which], hx, hy)

    def strip_copy(slot, side, which):
        to_hy = hy - 1 if side == 0 else hy + 1
        if which == 0:
            rows, target, sem, to_hx = packed.at[side, 0:8, :], strips.at[slot, 1 - side, 24:32, :], 2, hx - 1
        elif which == 1:
            rows, target, sem, to_hx = packed.at[side], strips.at[slot, 1 - side, 8:24, :], 1, hx
        else:
            rows, target, sem, to_hx = packed.at[side, 8:16, :], strips.at[slot, 1 - side, 0:8, :], 0, hx + 1
        return remote(rows, target, strip_send.at[side, which], strip_recv.at[slot, 1 - side, sem], to_hx, to_hy)

    def strip_arrival(slot, side, which):
        start, stop = ((0, 8), (8, 24), (24, 32))[which]
        rows = strips.at[slot, side, start:stop, :]
        return remote(rows, rows, strip_send.at[side, which], strip_recv.at[slot, side, which], hx, hy)

    def mixed_copy(slot):
        return remote(mixed_send, mixed_recv.at[slot], mixed_send_sem, mixed_recv_sem.at[slot], hx, beside_core)

    def partner_copy(slot):
        return remote(
            field.at[slot, own_rows, :], partner.at[slot], partner_send, partner_recv.at[slot], hx, beside_core
        )

    def on(conditions, action):
        if conditions:
            pl.when(functools.reduce(jnp.logical_and, conditions))(action)
        else:
            action()

    row_there = ((0, (up,)), (1, ()), (2, (down,)))
    side_there = ((0, left), (1, right))

    def tile_sends(slot, near, act):
        for distance in range(1, NEAR + 1) if near else range(GROUP - 1, NEAR, -1):
            for step in (-distance, distance):
                which = place + step
                on([which >= 0, which < GROUP], lambda which=which: act(tile_copy(slot, which, near)))

    def tile_waits(slot, near):
        for which in range(GROUP):
            distance = jnp.abs(place - which)
            chosen = [distance >= 1, distance <= NEAR] if near else [distance > NEAR]
            on(chosen, lambda which=which: tile_arrival(slot, which, near).wait_recv())

    def block_sends(slot, act):
        act(partner_copy(slot))
        tile_sends(slot, True, act)
        for side, beside in side_there:
            for which, there in row_there:
                on([beside, *there], lambda side=side, which=which: act(strip_copy(slot, side, which)))
        on([place == 0, up], lambda: act(edge_up(slot)))
        on([place == GROUP - 1, down], lambda: act(edge_down(slot)))

    def iteration(k, carry):
        slot = lax.rem(k, 2)
        block_sends(slot, lambda item: item.start())

        product = dot_split(split(field[slot, own_rows, :]), parts(col_parts.at[0]))
        partner_copy(slot).wait_recv()
        product = product + dot_split(split(partner[slot]), parts(col_parts.at[1]))
        products[slot, own_product, :] = product
        tile_sends(slot, False, lambda item: item.start())

        tile_waits(slot, True)
        mixed = dot_split(parts(row_near), split(field[slot, BAND : BAND + TILE, :]))
        mixed_send[...] = mixed
        mixed_copy(slot).start()
        total = dot_split(split(mixed), parts(col_parts.at[0]))

        on([place == 0, up], lambda: edge_arrival(slot, 0).wait_recv())
        on([place == GROUP - 1, down], lambda: edge_arrival(slot, 1).wait_recv())
        tall = field[slot, pl.ds(pl.multiple_of(place * ROWS, ROWS), LONG_ROWS), :]
        col_high, col_low = parts(col_forward)
        by_col = dot_split(split(tall), (col_high[0:COLS], col_low[0:COLS]))
        for side, beside in side_there:
            for which, there in row_there:
                on([beside, *there], lambda side=side, which=which: strip_arrival(slot, side, which).wait_recv())
        from_left, from_right = strips[slot, 0], strips[slot, 1]
        pieces = []
        for t in range(4):
            piece_left, piece_right = from_left[8 * t : 8 * t + 8, :], from_right[8 * t : 8 * t + 8, :]
            for g in range(4):
                piece = jnp.where(
                    lane_group == g, piece_right, jnp.where(lane_group == (g + 3) % 4, piece_left, 0.0)
                )
                pieces.append(pltpu.roll(piece, COLS - BAND * g, axis=1) if g else piece)
        outside = jnp.concatenate(pieces, axis=0)
        by_col = by_col + dot_split(split(outside), (col_high[COLS:], col_low[COLS:]))
        turned = dot_split(parts(row_forward), split(by_col))
        freq_re = turned[0:LONG_ROWS, 0:COLS] + turned[LONG_ROWS:, COLS:]
        freq_im = turned[0:LONG_ROWS, COLS:] - turned[LONG_ROWS:, 0:COLS]
        c_re, c_im = coeff_re[...], coeff_im[...]
        shaped = jnp.concatenate([freq_re * c_re - freq_im * c_im, freq_re * c_im + freq_im * c_re], axis=1)
        turned = dot_split(parts(row_inverse), split(shaped))
        back = jnp.concatenate(
            [turned[0:ROWS, 0:COLS] - turned[ROWS:, COLS:], turned[0:ROWS, COLS:] + turned[ROWS:, 0:COLS]], axis=1
        )
        total = total + dot_split(split(back), parts(col_inverse))

        mixed_copy(slot).wait_recv()
        total = total + dot_split(split(mixed_recv[slot]), parts(col_parts.at[1]))
        tile_waits(slot, False)
        total = total + dot_split(parts(row_far), split(products[slot]))

        keep = jnp.where(k == 0, 0.0, 1.0 - STEP)
        take = jnp.where(k == 0, 1.0, STEP)
        residual = keep * field[slot, own_rows, :] - take * total
        block_sends(slot, lambda item: item.wait_send())
        tile_sends(slot, False, lambda item: item.wait_send())
        mixed_copy(slot).wait_send()
        field[1 - slot, own_rows, :] = residual
        pack(residual)
        accum[...] += STEP * residual
        squares[pl.ds(k, 1), :] = jnp.sum(residual * residual, axis=0, keepdims=True)
        return carry

    lax.fori_loop(0, ITERS, iteration, 0)
    out_ref[...] = accum[...]

    def gather(total, held, recv_sem, index, size, device):
        held[index] = total

        def copy(to, at):
            return remote(
                held.at[index], held.at[at], sum_send.at[to], recv_sem.at[at], *device(to)
            )

        def start(i, carry):
            copy(lax.rem(index + i, size), index).start()
            return carry

        def wait(i, carry):
            other = lax.rem(index + i, size)
            item = remote(held.at[other], held.at[other], sum_send.at[other], recv_sem.at[other], *device(other))
            item.wait_recv()
            copy(other, index).wait_send()
            return carry

        lax.fori_loop(1, size, start, 0)
        lax.fori_loop(1, size, wait, 0)
        return jnp.sum(held[...], axis=0)

    total = gather(squares[...], sum_y, sum_y_recv, hy, n_hy, lambda to: (hx, to))
    total = gather(total, sum_z, sum_z_recv, z, n_z, lambda to: (x * n_z + to, hy))
    if n_x > 1:
        total = gather(total, sum_x, sum_x_recv, x, n_x, lambda to: (to * n_z + z, hy))
    mean = jnp.sum(total, axis=1, keepdims=True) / (ROWS * COLS * n_hx * n_hy)
    norm_ref[...] = jnp.broadcast_to(jnp.sqrt(mean + TINY), norm_ref.shape)


def local_step(sizes, source, coeffs, row_factor, col_factor, tile_mask):
    n_hx, n_hy, n_z = sizes
    constants = [jnp.asarray(t) for t in tables()]
    any_spec = pl.BlockSpec(memory_space=pl.ANY)
    vmem_spec = pl.BlockSpec(memory_space=pltpu.VMEM)
    dma = pltpu.SemaphoreType.DMA
    taps = 2 * BAND + 1
    scratch = [
        pltpu.VMEM((2, TILE + 2 * BAND, COLS), F32),
        pltpu.VMEM((2, TILE, COLS), F32),
        pltpu.VMEM((2, ROWS, COLS), F32),
        pltpu.VMEM((2, 2, 32, COLS), F32),
        pltpu.VMEM((2, 16, COLS), F32),
        pltpu.VMEM((ROWS, COLS), F32),
        pltpu.VMEM((2, ROWS, COLS), F32),
        pltpu.VMEM((ROWS, COLS), F32),
        pltpu.VMEM((ITERS, COLS), F32),
        pltpu.VMEM((taps, taps), F32),
        pltpu.VMEM((LONG_ROWS, COLS), F32),
        pltpu.VMEM((ROWS, TILE), F32),
        pltpu.VMEM((TILE, COLS), F32),
        pltpu.VMEM((2 * ROWS, TILE), BF16),
        pltpu.VMEM((2 * ROWS, TILE), BF16),
        pltpu.VMEM((2, 2 * COLS, COLS), BF16),
        pltpu.VMEM((LONG_ROWS, COLS), F32),
        pltpu.VMEM((LONG_ROWS, COLS), F32),
        *[pltpu.VMEM(c.shape, c.dtype) for c in constants],
        pltpu.VMEM((n_hy, ITERS, COLS), F32),
        pltpu.VMEM((n_z, ITERS, COLS), F32),
        pltpu.VMEM((n_hx // n_z, ITERS, COLS), F32),
        dma((9,)),
        dma((GROUP,)), dma((2, GROUP)),
        dma, dma((2,)),
        dma((2,)), dma((2, 2)),
        dma((2, 3)), dma((2, 2, 3)),
        dma, dma((2,)),
        dma((max(n_hy, n_z),)), dma((n_hy,)), dma((n_z,)), dma((n_hx // n_z,)),
    ]
    result, norms = pl.pallas_call(
        functools.partial(kernel, sizes),
        out_shape=(jax.ShapeDtypeStruct((ROWS, COLS), F32), jax.ShapeDtypeStruct((ITERS, COLS), F32)),
        in_specs=[any_spec] * 4 + [pl.BlockSpec(memory_space=pltpu.SMEM)] + [any_spec] * 5,
        out_specs=(vmem_spec, vmem_spec),
        scratch_shapes=scratch,
        compiler_params=pltpu.CompilerParams(collective_id=0, has_side_effects=True),
        name="richardson",
    )(source, coeffs, row_factor, col_factor, tile_mask, *constants)
    return result, norms[:, 0]


def solution(mesh):
    n_hx, n_hy = mesh.shape["hx"], mesh.shape["hy"]
    sizes = (n_hx, n_hy, min(n_hx, Z_SIZE))
    in_specs = (P("hx", "hy"), P(), P("hx", None), P(None, "hy"), P())
    out_specs = (P("hx", "hy"), P())
    return jax.shard_map(
        functools.partial(local_step, sizes), mesh=mesh, in_specs=in_specs, out_specs=out_specs, check_vma=False
    )
```

```python
import functools

import jax
import jax.numpy as jnp
import ml_dtypes
import numpy as np
from jax import lax
from jax.experimental import pallas as pl
from jax.experimental.pallas import tpu as pltpu
from jax.sharding import PartitionSpec as P

TILE = 256
BAND = 32
ITERS = 8
ROWS = 64
COLS = 128
GROUP = TILE // ROWS
LONG_ROWS = ROWS + 2 * BAND
LONG_COLS = COLS + 2 * BAND
HALF = LONG_COLS // 2 + 1
NEAR = 1
STEP = 0.25
TINY = 1e-06
Z_SIZE = 8
MESH = pl.DeviceIdType.MESH
F32 = jnp.float32
BF16 = jnp.bfloat16


def split_table(table):
    high = table.astype(np.float32).astype(ml_dtypes.bfloat16)
    low = (table - high.astype(np.float64)).astype(np.float32).astype(ml_dtypes.bfloat16)
    return high, low


def tables():
    lane = np.arange(COLS)
    freq_col = np.arange(COLS)
    kept = (freq_col < HALF).astype(np.float64)
    place = np.concatenate([lane + BAND, np.where(lane < BAND, lane + BAND + COLS, lane - (COLS - BAND))])
    used = np.concatenate([np.ones(COLS), ((lane < BAND) | (lane >= COLS - BAND)).astype(np.float64)])
    angle = 2 * np.pi * ((place[:, None] * freq_col[None, :]) % LONG_COLS) / LONG_COLS
    weight = used[:, None] * kept[None, :]
    col_forward = np.concatenate([np.cos(angle) * weight, -np.sin(angle) * weight], axis=1)
    tap = np.arange(LONG_ROWS)
    angle = 2 * np.pi * ((tap[:, None] * freq_col[None, :]) % LONG_COLS) / LONG_COLS
    weight = (tap <= 2 * BAND)[:, None] * kept[None, :]
    coeff_forward = np.concatenate([np.cos(angle) * weight, -np.sin(angle) * weight], axis=1)
    row = np.arange(LONG_ROWS)
    angle = 2 * np.pi * ((row[:, None] * row[None, :]) % LONG_ROWS) / LONG_ROWS
    order = np.concatenate([row[0::2], row[1::2]])
    halves = [angle[row[odd::2], : LONG_ROWS // 2] for odd in (0, 1)]
    row_forward = np.concatenate([f(half) for half in halves for f in (np.cos, np.sin)], axis=0)
    target = np.arange(ROWS) + 2 * BAND
    angle = 2 * np.pi * ((target[:, None] * order[None, :]) % LONG_ROWS) / LONG_ROWS
    row_inverse = np.concatenate([np.cos(angle), np.sin(angle)], axis=0)
    target = lane + 2 * BAND
    angle = 2 * np.pi * ((freq_col[:, None] * target[None, :]) % LONG_COLS) / LONG_COLS
    scale = np.where((freq_col == 0) | (freq_col == HALF - 1), 1.0, 2.0) * kept / (LONG_ROWS * LONG_COLS)
    col_inverse = np.concatenate([np.cos(angle) * scale[:, None], -np.sin(angle) * scale[:, None]], axis=0)
    high, low = split_table(row_forward)
    row_forward = np.concatenate([high, high, low, low], axis=1)
    return [
        np.concatenate(split_table(col_forward), axis=0),
        np.concatenate(split_table(coeff_forward), axis=0),
        row_forward,
        np.concatenate(split_table(row_inverse), axis=1),
        np.concatenate(split_table(col_inverse), axis=1),
    ]


def split(value):
    high = value.astype(BF16)
    return high, (value - high.astype(F32)).astype(BF16)


def dot(a, b):
    return jnp.dot(a, b, preferred_element_type=F32)


def beside(*values):
    return jnp.concatenate(values, axis=1)


def below(*values):
    return jnp.concatenate(values, axis=0)


def dot_rows(a, b):
    (a_high, a_low), (b_high, b_low) = a, b
    both = dot(below(a_high, a_low), b_high)
    count = a_high.shape[0]
    return both[0:count] + both[count:] + dot(a_high, b_low)


def dot_small(a, b):
    both = dot(a, b)
    return both[:, 0:COLS] + both[:, COLS:]


def dot_deep(a, b):
    both = dot(a, b)
    count = a.shape[0] // 2
    return both[0:count, 0:COLS] + (both[0:count, COLS:] + both[count:, 0:COLS])


def transform_rows(value, table):
    half = LONG_ROWS // 2
    top, bottom = value[0:half], value[half:]
    parts_re, parts_im = [], []
    for at, both in ((0, top + bottom), (LONG_ROWS, top - bottom)):
        high, low = split(both)
        turned = dot(table[at : at + LONG_ROWS, :], below(high, low, high, low))
        cosine, sine = turned[0:half], turned[half:]
        parts_re.append(cosine[:, 0:COLS] + sine[:, COLS:])
        parts_im.append(cosine[:, COLS:] - sine[:, 0:COLS])
    return below(*parts_re), below(*parts_im)


def parts(ref):
    half = ref.shape[0] // 2
    return ref[0:half, :], ref[half:, :]


def kernel(
    sizes,
    source_hbm, coeffs_hbm, row_hbm, col_hbm, mask_hbm,
    col_forward_hbm, coeff_forward_hbm, row_forward_hbm, row_inverse_hbm, col_inverse_hbm,
    out_ref, norm_ref,
    field, product_send, far, partner, strips, packed, mixed_send, mixed_recv, accum, squares,
    mask, coeffs_raw, coeffs_pad, row_tile, col_tile, row_near, row_far, col_parts, coeff_re, coeff_im,
    col_forward, coeff_forward, row_forward, row_inverse, col_inverse,
    sum_y, sum_x,
    local_sem, tile_send, tile_recv, partner_send, partner_recv, edge_send, edge_recv, strip_send, strip_recv,
    mixed_send_sem, mixed_recv_sem, sum_send, sum_y_recv, sum_x_recv,
):
    n_hx, n_hy = sizes
    n_z = min(n_hx, Z_SIZE)
    n_x = n_hx // n_z
    hx, hy = lax.axis_index("hx"), lax.axis_index("hy")
    place = lax.rem(hx, GROUP)
    first = hx - place
    tile_row, tile_col = hx // GROUP, hy // 2
    core = lax.rem(hy, 2)
    x, z = hx // n_z, lax.rem(hx, n_z)
    up, down, left, right = hx > 0, hx < n_hx - 1, hy > 0, hy < n_hy - 1
    own_rows = pl.ds(pl.multiple_of(BAND + place * ROWS, BAND), ROWS)
    own_far = pl.ds(pl.multiple_of(lax.rem(place, 2) * ROWS, ROWS), ROWS)
    far_first = jnp.where(place < 2, 2, 0)
    beside_core = hy + 1 - 2 * core

    for slot in range(2):
        field[slot] = jnp.zeros(field.shape[1:], F32)
        far[slot] = jnp.zeros(far.shape[1:], F32)
        for side in range(2):
            strips[slot, side] = jnp.zeros((4 * 8, COLS), F32)
    coeffs_pad[...] = jnp.zeros_like(coeffs_pad)

    local = [
        pltpu.make_async_copy(source_hbm, field.at[0, own_rows, :], local_sem.at[0]),
        pltpu.make_async_copy(coeffs_hbm, coeffs_raw, local_sem.at[1]),
        pltpu.make_async_copy(
            row_hbm.at[:, pl.ds(pl.multiple_of(tile_col * TILE, TILE), TILE)], row_tile, local_sem.at[2]
        ),
        pltpu.make_async_copy(
            col_hbm.at[pl.ds(pl.multiple_of(tile_row * TILE, TILE), TILE), :], col_tile, local_sem.at[3]
        ),
        pltpu.make_async_copy(col_forward_hbm, col_forward, local_sem.at[4]),
        pltpu.make_async_copy(coeff_forward_hbm, coeff_forward, local_sem.at[5]),
        pltpu.make_async_copy(row_forward_hbm, row_forward, local_sem.at[6]),
        pltpu.make_async_copy(row_inverse_hbm, row_inverse, local_sem.at[7]),
        pltpu.make_async_copy(col_inverse_hbm, col_inverse, local_sem.at[8]),
        pltpu.make_async_copy(mask_hbm, mask, local_sem.at[9]),
    ]
    for item in local:
        item.start()

    barrier = pltpu.get_barrier_semaphore()

    def greet(to_hx, to_hy):
        pl.semaphore_signal(barrier, inc=1, device_id=(to_hx, to_hy), device_id_type=MESH)

    def greet_y(i, carry):
        greet(hx, lax.rem(hy + i, n_hy))
        return carry

    def greet_z(i, carry):
        greet(x * n_z + lax.rem(z + i, n_z), hy)
        return carry

    def greet_x(i, carry):
        greet(lax.rem(x + i, n_x) * n_z + z, hy)
        return carry

    lax.fori_loop(1, n_hy, greet_y, 0)
    lax.fori_loop(1, n_z, greet_z, 0)
    lax.fori_loop(1, n_x, greet_x, 0)
    for there, to_hx in ((up, hx - 1), (down, hx + 1)):
        @pl.when(there)
        def _():
            greet(to_hx, hy)

            @pl.when(left)
            def _():
                greet(to_hx, hy - 1)

            @pl.when(right)
            def _():
                greet(to_hx, hy + 1)

    lane_group = lax.broadcasted_iota(jnp.int32, (8, COLS), 1) // BAND

    def pack(slot, value):
        for half in range(2):
            to_left = to_right = None
            for g in range(4):
                start = half * BAND + 8 * g
                rolled = value[start : start + 8, :]
                if g:
                    rolled = pltpu.roll(rolled, BAND * g, axis=1)
                if to_left is None:
                    to_left = to_right = rolled
                else:
                    to_left = jnp.where(lane_group == g, rolled, to_left)
                    to_right = jnp.where(lane_group == (g + 3) % 4, rolled, to_right)
            packed[slot, 0, 8 * half : 8 * half + 8, :] = to_left
            packed[slot, 1, 8 * half : 8 * half + 8, :] = to_right

    local[0].wait()
    accum[...] = jnp.zeros_like(accum)

    count = (up.astype(jnp.int32) + down.astype(jnp.int32)) * (
        1 + left.astype(jnp.int32) + right.astype(jnp.int32)
    ) + (n_hy - 1 + n_z - 1 + n_x - 1)
    pl.semaphore_wait(barrier, count)

    def prepare():
        local[2].wait()
        local[3].wait()
        local[9].wait()
        active = mask[tile_row, tile_col].astype(F32)
        def distance(width, start):
            return jnp.abs(lax.broadcasted_iota(jnp.int32, (ROWS, width), 1) // ROWS + (start - place))

        far_cols = row_tile[:, pl.ds(pl.multiple_of(far_first * ROWS, 2 * ROWS), 2 * ROWS)]
        for parts_of, value, chosen in (
            (row_near, row_tile[...], distance(TILE, 0) <= NEAR),
            (row_far, far_cols, distance(2 * ROWS, far_first) > NEAR),
        ):
            high, low = split(jnp.where(chosen, value * active, 0.0))
            parts_of[...] = below(high, low) if parts_of is row_near else beside(high, low)
        for which, start in enumerate((core, 1 - core)):
            high, low = split(col_tile[pl.ds(pl.multiple_of(start * COLS, COLS), COLS), :])
            col_parts[which, 0:COLS, :] = beside(high, low)
            col_parts[which, COLS:, :] = beside(high, low)
        local[1].wait()
        coeffs_pad[0 : 2 * BAND + 1, 0 : 2 * BAND + 1] = coeffs_raw[...]
        local[5].wait()
        local[6].wait()
        by_col = dot_rows(split(coeffs_pad[...]), parts(coeff_forward))
        coeff_re[...], coeff_im[...] = transform_rows(by_col, row_forward)
        for i in (4, 7, 8):
            local[i].wait()

    def remote(source_ref, target_ref, send_sem, recv_sem, to_hx, to_hy):
        return pltpu.make_async_remote_copy(
            src_ref=source_ref, dst_ref=target_ref, send_sem=send_sem, recv_sem=recv_sem,
            device_id=(to_hx, to_hy), device_id_type=MESH,
        )

    def tile_copy(slot, which, near):
        block = field.at[slot, own_rows, :]
        source_ref, target_ref = (block, block) if near else (product_send.at[slot], far.at[slot, own_far, :])
        return remote(source_ref, target_ref, tile_send.at[slot, which], tile_recv.at[slot, place], first + which, hy)

    def tile_arrival(slot, which, near):
        if near:
            block = field.at[slot, BAND + which * ROWS : BAND + (which + 1) * ROWS, :]
        else:
            block = far.at[slot, which % 2 * ROWS : (which % 2 + 1) * ROWS, :]
        return remote(block, block, tile_send.at[slot, which], tile_recv.at[slot, which], first + which, hy)

    def edge_up(slot):
        return remote(
            field.at[slot, BAND : 2 * BAND, :], field.at[slot, BAND + TILE : 2 * BAND + TILE, :],
            edge_send.at[slot, 0], edge_recv.at[slot, 1], hx - 1, hy,
        )

    def edge_down(slot):
        return remote(
            field.at[slot, TILE : TILE + BAND, :], field.at[slot, 0:BAND, :],
            edge_send.at[slot, 1], edge_recv.at[slot, 0], hx + 1, hy,
        )

    def edge_arrival(slot, which):
        rows = field.at[slot, 0:BAND, :] if which == 0 else field.at[slot, BAND + TILE : 2 * BAND + TILE, :]
        return remote(rows, rows, edge_send.at[slot, which], edge_recv.at[slot, which], hx, hy)

    def strip_copy(slot, side, which):
        to_hy = hy - 1 if side == 0 else hy + 1
        if which == 0:
            rows, target, sem, to_hx = packed.at[slot, side, 0:8, :], strips.at[slot, 1 - side, 24:32, :], 2, hx - 1
        elif which == 1:
            rows, target, sem, to_hx = packed.at[slot, side], strips.at[slot, 1 - side, 8:24, :], 1, hx
        else:
            rows, target, sem, to_hx = packed.at[slot, side, 8:16, :], strips.at[slot, 1 - side, 0:8, :], 0, hx + 1
        return remote(rows, target, strip_send.at[slot, side, which], strip_recv.at[slot, 1 - side, sem], to_hx, to_hy)

    def strip_arrival(slot, side, which):
        start, stop = ((0, 8), (8, 24), (24, 32))[which]
        rows = strips.at[slot, side, start:stop, :]
        return remote(rows, rows, strip_send.at[slot, side, which], strip_recv.at[slot, side, which], hx, hy)

    def mixed_copy(slot):
        return remote(mixed_send.at[slot], mixed_recv.at[slot], mixed_send_sem.at[slot], mixed_recv_sem.at[slot], hx, beside_core)

    def partner_copy(slot):
        return remote(
            field.at[slot, own_rows, :], partner.at[slot], partner_send.at[slot], partner_recv.at[slot], hx, beside_core
        )

    def on(conditions, action):
        if conditions:
            pl.when(functools.reduce(jnp.logical_and, conditions))(action)
        else:
            action()

    row_there = ((0, (up,)), (1, ()), (2, (down,)))
    side_there = ((0, left), (1, right))

    def tile_sends(slot, near, act):
        for distance in range(1, NEAR + 1) if near else range(GROUP - 1, NEAR, -1):
            for step in (-distance, distance):
                which = place + step
                on([which >= 0, which < GROUP], lambda which=which: act(tile_copy(slot, which, near)))

    def tile_waits(slot, near):
        for which in range(GROUP):
            distance = jnp.abs(place - which)
            chosen = [distance >= 1, distance <= NEAR] if near else [distance > NEAR]
            on(chosen, lambda which=which: tile_arrival(slot, which, near).wait_recv())

    def edge_sends(slot, act):
        on([place == 0, up], lambda: act(edge_up(slot)))
        on([place == GROUP - 1, down], lambda: act(edge_down(slot)))

    def strip_sends(slot, act):
        for which, there in (row_there[0], row_there[2], row_there[1]):
            for side, next_to in side_there:
                on([next_to, *there], lambda side=side, which=which: act(strip_copy(slot, side, which)))

    def gain(k, value):
        accum[...] += jnp.where(k == 0, 1.0, STEP) * value
        squares[pl.ds(k + ITERS - 1, 1), :] = jnp.sum(value * value, axis=0, keepdims=True)

    def begin(item):
        item.start()

    def finish(item):
        item.wait_send()

    def all_sent(slot):
        partner_copy(slot).wait_send()
        mixed_copy(slot).wait_send()
        edge_sends(slot, finish)
        tile_sends(slot, True, finish)
        strip_sends(slot, finish)
        tile_sends(slot, False, finish)

    def iteration(k, carry):
        slot = lax.rem(k, 2)
        partner_copy(slot).start()
        edge_sends(slot, begin)
        tile_sends(slot, True, begin)
        value = field[slot, own_rows, :]
        pack(slot, value)
        strip_sends(slot, begin)

        pl.when(k == 0)(prepare)

        product = dot_small(beside(*split(value)), col_parts[0])
        gain(k, value)
        partner_copy(slot).wait_recv()
        product_send[slot] = product + dot_small(beside(*split(partner[slot])), col_parts[1])
        tile_sends(slot, False, begin)

        tile_waits(slot, True)
        mixed = dot_deep(row_near[...], beside(*split(field[slot, BAND : BAND + TILE, :])))
        mixed_send[slot] = mixed
        mixed_copy(slot).start()
        total = dot_small(beside(*split(mixed)), col_parts[0])

        on([place == 0, up], lambda: edge_arrival(slot, 0).wait_recv())
        on([place == GROUP - 1, down], lambda: edge_arrival(slot, 1).wait_recv())
        tall = field[slot, pl.ds(pl.multiple_of(place * ROWS, ROWS), LONG_ROWS), :]
        for side, next_to in side_there:
            for which, there in row_there:
                on([next_to, *there], lambda side=side, which=which: strip_arrival(slot, side, which).wait_recv())
        from_left, from_right = strips[slot, 0], strips[slot, 1]
        pieces = []
        for t in range(4):
            piece_left, piece_right = from_left[8 * t : 8 * t + 8, :], from_right[8 * t : 8 * t + 8, :]
            for g in range(4):
                piece = jnp.where(
                    lane_group == g, piece_right, jnp.where(lane_group == (g + 3) % 4, piece_left, 0.0)
                )
                pieces.append(pltpu.roll(piece, COLS - BAND * g, axis=1) if g else piece)
        by_col = dot_rows(split(beside(tall, below(*pieces))), parts(col_forward))
        freq_re, freq_im = transform_rows(by_col, row_forward)
        c_re, c_im = coeff_re[...], coeff_im[...]
        high, low = split(beside(freq_re * c_re - freq_im * c_im, freq_re * c_im + freq_im * c_re))
        turned = dot(row_inverse[...], below(high, high)) + dot(row_inverse[:, 0:LONG_ROWS], low)
        cosine, sine = turned[0:ROWS], turned[ROWS:]
        back = beside(cosine[:, 0:COLS] - sine[:, COLS:], cosine[:, COLS:] + sine[:, 0:COLS])
        total = total + dot_deep(below(*split(back)), col_inverse[...])

        mixed_copy(slot).wait_recv()
        total = total + dot_small(beside(*split(mixed_recv[slot])), col_parts[1])
        pl.when(k > 0)(lambda: all_sent(1 - slot))
        keep = jnp.where(k == 0, 0.0, 1.0 - STEP)
        take = jnp.where(k == 0, 1.0, STEP)
        total = keep * value - take * total
        tile_waits(slot, False)
        field[1 - slot, own_rows, :] = total - take * dot_small(row_far[...], below(*[beside(*split(far[slot]))] * 2))
        return carry

    lax.fori_loop(0, ITERS, iteration, 0)
    gain(ITERS, field[ITERS % 2, own_rows, :])
    out_ref[...] = accum[...]
    all_sent((ITERS - 1) % 2)

    def gather(total, held, recv_sem, index, size, device):
        held[index] = total

        def copy(to, at):
            return remote(
                held.at[index], held.at[at], sum_send.at[to], recv_sem.at[at], *device(to)
            )

        def start(i, carry):
            copy(lax.rem(index + i, size), index).start()
            return carry

        def wait(i, carry):
            other = lax.rem(index + i, size)
            item = remote(held.at[other], held.at[other], sum_send.at[other], recv_sem.at[other], *device(other))
            item.wait_recv()
            copy(other, index).wait_send()
            return carry

        lax.fori_loop(1, size, start, 0)
        lax.fori_loop(1, size, wait, 0)
        return jnp.sum(held[...], axis=0)

    total = gather(squares[ITERS:, :], sum_y, sum_y_recv, hy, n_hy, lambda to: (hx, to))
    total = gather(total, sum_x.at[0:n_z], sum_x_recv.at[0], z, n_z, lambda to: (x * n_z + to, hy))
    if n_x > 1:
        total = gather(total, sum_x.at[n_z : n_z + n_x], sum_x_recv.at[1], x, n_x, lambda to: (to * n_z + z, hy))
    mean = jnp.sum(total, axis=1, keepdims=True) / (ROWS * COLS * n_hx * n_hy)
    norm_ref[...] = jnp.broadcast_to(jnp.sqrt(mean + TINY), norm_ref.shape)


def local_step(sizes, source, coeffs, row_factor, col_factor, tile_mask):
    n_hx, n_hy = sizes
    constants = [jnp.asarray(t) for t in tables()]
    any_spec = pl.BlockSpec(memory_space=pl.ANY)
    vmem_spec = pl.BlockSpec(memory_space=pltpu.VMEM)
    dma = pltpu.SemaphoreType.DMA
    taps = 2 * BAND + 1
    scratch = [
        pltpu.VMEM((2, TILE + 2 * BAND, COLS), F32),
        pltpu.VMEM((2, ROWS, COLS), F32),
        pltpu.VMEM((2, 2 * ROWS, COLS), F32),
        pltpu.VMEM((2, ROWS, COLS), F32),
        pltpu.VMEM((2, 2, 32, COLS), F32),
        pltpu.VMEM((2, 2, 16, COLS), F32),
        pltpu.VMEM((2, ROWS, COLS), F32),
        pltpu.VMEM((2, ROWS, COLS), F32),
        pltpu.VMEM((ROWS, COLS), F32),
        pltpu.VMEM((2 * ITERS, COLS), F32),
        pltpu.SMEM((n_hx // GROUP, n_hy // 2), jnp.int32),
        pltpu.VMEM((taps, taps), F32),
        pltpu.VMEM((LONG_ROWS, COLS), F32),
        pltpu.VMEM((ROWS, TILE), F32),
        pltpu.VMEM((TILE, COLS), F32),
        pltpu.VMEM((2 * ROWS, TILE), BF16),
        pltpu.VMEM((ROWS, 4 * ROWS), BF16),
        pltpu.VMEM((2, 2 * COLS, 2 * COLS), BF16),
        pltpu.VMEM((LONG_ROWS, COLS), F32),
        pltpu.VMEM((LONG_ROWS, COLS), F32),
        *[pltpu.VMEM(c.shape, c.dtype) for c in constants],
        pltpu.VMEM((n_hy, ITERS, COLS), F32),
        pltpu.VMEM((n_hx, ITERS, COLS), F32),
        dma((10,)),
        dma((2, GROUP)), dma((2, GROUP)),
        dma((2,)), dma((2,)),
        dma((2, 2)), dma((2, 2)),
        dma((2, 2, 3)), dma((2, 2, 3)),
        dma((2,)), dma((2,)),
        dma((max(n_hy, n_hx),)), dma((n_hy,)), dma((2, n_hx)),
    ]
    result, norms = pl.pallas_call(
        functools.partial(kernel, sizes),
        out_shape=(pltpu.VMEM((ROWS, COLS), F32), pltpu.VMEM((ITERS, COLS), F32)),
        in_specs=[any_spec] * 10,
        out_specs=(vmem_spec, vmem_spec),
        scratch_shapes=scratch,
        compiler_params=pltpu.CompilerParams(collective_id=0, has_side_effects=True),
        name="richardson",
    )(source, coeffs, row_factor, col_factor, tile_mask, *constants)
    return result, norms[:, 0]


def solution(mesh):
    n_hx, n_hy = mesh.shape["hx"], mesh.shape["hy"]
    sizes = (n_hx, n_hy)
    in_specs = (P("hx", "hy"), P(), P("hx", None), P(None, "hy"), P())
    out_specs = (P("hx", "hy"), P())
    return jax.shard_map(
        functools.partial(local_step, sizes), mesh=mesh, in_specs=in_specs, out_specs=out_specs, check_vma=False
    )
```

```python
import functools

import jax
import jax.numpy as jnp
import ml_dtypes
import numpy as np
from jax import lax
from jax.experimental import pallas as pl
from jax.experimental.pallas import tpu as pltpu
from jax.sharding import PartitionSpec as P

TILE = 256
BAND = 32
ITERS = 8
ROWS = 64
COLS = 128
GROUP = TILE // ROWS
LONG_ROWS = ROWS + 2 * BAND
LONG_COLS = COLS + 2 * BAND
HALF = LONG_COLS // 2 + 1
NEAR = 1
STEP = 0.25
TINY = 1e-06
Z_SIZE = 8
MESH = pl.DeviceIdType.MESH
F32 = jnp.float32
BF16 = jnp.bfloat16


def split_table(table):
    high = table.astype(np.float32).astype(ml_dtypes.bfloat16)
    low = (table - high.astype(np.float64)).astype(np.float32).astype(ml_dtypes.bfloat16)
    return high, low


def tables():
    lane = np.arange(COLS)
    freq_col = np.arange(COLS)
    kept = (freq_col < HALF).astype(np.float64)
    place = np.concatenate([lane + BAND, np.where(lane < BAND, lane + BAND + COLS, lane - (COLS - BAND))])
    used = np.concatenate([np.ones(COLS), ((lane < BAND) | (lane >= COLS - BAND)).astype(np.float64)])
    angle = 2 * np.pi * ((place[:, None] * freq_col[None, :]) % LONG_COLS) / LONG_COLS
    weight = used[:, None] * kept[None, :]
    col_forward = np.concatenate([np.cos(angle) * weight, -np.sin(angle) * weight], axis=1)
    tap = np.arange(LONG_ROWS)
    angle = 2 * np.pi * ((tap[:, None] * freq_col[None, :]) % LONG_COLS) / LONG_COLS
    weight = (tap <= 2 * BAND)[:, None] * kept[None, :]
    coeff_forward = np.concatenate([np.cos(angle) * weight, -np.sin(angle) * weight], axis=1)
    row = np.arange(LONG_ROWS)
    angle = 2 * np.pi * ((row[:, None] * row[None, :]) % LONG_ROWS) / LONG_ROWS
    order = np.concatenate([row[0::2], row[1::2]])
    halves = [angle[row[odd::2], : LONG_ROWS // 2] for odd in (0, 1)]
    row_forward = np.concatenate([f(half) for half in halves for f in (np.cos, np.sin)], axis=0)
    target = np.arange(ROWS) + 2 * BAND
    angle = 2 * np.pi * ((target[:, None] * order[None, :]) % LONG_ROWS) / LONG_ROWS
    row_inverse = np.concatenate([np.cos(angle), np.sin(angle)], axis=0)
    target = lane + 2 * BAND
    angle = 2 * np.pi * ((freq_col[:, None] * target[None, :]) % LONG_COLS) / LONG_COLS
    scale = np.where((freq_col == 0) | (freq_col == HALF - 1), 1.0, 2.0) * kept / (LONG_ROWS * LONG_COLS)
    col_inverse = np.concatenate([np.cos(angle) * scale[:, None], -np.sin(angle) * scale[:, None]], axis=0)
    high, low = split_table(row_forward)
    row_forward = np.concatenate([high, high, low, low], axis=1)
    return [
        np.concatenate(split_table(col_forward), axis=0),
        np.concatenate(split_table(coeff_forward), axis=0),
        row_forward,
        np.concatenate(split_table(row_inverse), axis=1),
        np.concatenate(split_table(col_inverse), axis=1),
    ]


def split(value):
    high = value.astype(BF16)
    return high, (value - high.astype(F32)).astype(BF16)


def dot(a, b):
    return jnp.dot(a, b, preferred_element_type=F32)


def beside(*values):
    return jnp.concatenate(values, axis=1)


def below(*values):
    return jnp.concatenate(values, axis=0)


def dot_rows(a, b):
    (a_high, a_low), (b_high, b_low) = a, b
    both = dot(below(a_high, a_low), b_high)
    count = a_high.shape[0]
    return both[0:count] + both[count:] + dot(a_high, b_low)


def dot_small(a, b):
    both = dot(a, b)
    return both[:, 0:COLS] + both[:, COLS:]


def dot_deep(a, b):
    both = dot(a, b)
    count = a.shape[0] // 2
    return both[0:count, 0:COLS] + (both[0:count, COLS:] + both[count:, 0:COLS])


def transform_rows(value, table):
    half = LONG_ROWS // 2
    top, bottom = value[0:half], value[half:]
    parts_re, parts_im = [], []
    for at, both in ((0, top + bottom), (LONG_ROWS, top - bottom)):
        high, low = split(both)
        turned = dot(table[at : at + LONG_ROWS, :], below(high, low, high, low))
        cosine, sine = turned[0:half], turned[half:]
        parts_re.append(cosine[:, 0:COLS] + sine[:, COLS:])
        parts_im.append(cosine[:, COLS:] - sine[:, 0:COLS])
    return below(*parts_re), below(*parts_im)


def parts(ref):
    half = ref.shape[0] // 2
    return ref[0:half, :], ref[half:, :]


def kernel(
    sizes,
    source_hbm, coeffs_hbm, row_hbm, col_hbm, mask_hbm,
    col_forward_hbm, coeff_forward_hbm, row_forward_hbm, row_inverse_hbm, col_inverse_hbm,
    out_ref, norm_ref,
    field, product_send, far, partner, strips, packed, mixed_send, mixed_recv, accum, squares,
    mask, coeffs_raw, coeffs_pad, row_tile, col_tile, row_near, row_far, col_parts, coeff_re, coeff_im,
    col_forward, coeff_forward, row_forward, row_inverse, col_inverse,
    sum_y, sum_x,
    local_sem, tile_send, tile_recv, partner_send, partner_recv, edge_send, edge_recv, strip_send, strip_recv,
    mixed_send_sem, mixed_recv_sem, sum_send, sum_y_recv, sum_x_recv,
):
    n_hx, n_hy = sizes
    n_z = min(n_hx, Z_SIZE)
    n_x = n_hx // n_z
    hx, hy = lax.axis_index("hx"), lax.axis_index("hy")
    place = lax.rem(hx, GROUP)
    first = hx - place
    tile_row, tile_col = hx // GROUP, hy // 2
    core = lax.rem(hy, 2)
    x, z = hx // n_z, lax.rem(hx, n_z)
    up, down, left, right = hx > 0, hx < n_hx - 1, hy > 0, hy < n_hy - 1
    own_rows = pl.ds(pl.multiple_of(BAND + place * ROWS, BAND), ROWS)
    own_far = pl.ds(pl.multiple_of(lax.rem(place, 2) * ROWS, ROWS), ROWS)
    far_first = jnp.where(place < 2, 2, 0)
    beside_core = hy + 1 - 2 * core

    for slot in range(2):
        field[slot] = jnp.zeros(field.shape[1:], F32)
        far[slot] = jnp.zeros(far.shape[1:], F32)
        for side in range(2):
            strips[slot, side] = jnp.zeros((4 * 8, COLS), F32)
    coeffs_pad[...] = jnp.zeros_like(coeffs_pad)

    local = [
        pltpu.make_async_copy(source_hbm, field.at[0, own_rows, :], local_sem.at[0]),
        pltpu.make_async_copy(coeffs_hbm, coeffs_raw, local_sem.at[1]),
        pltpu.make_async_copy(
            row_hbm.at[:, pl.ds(pl.multiple_of(tile_col * TILE, TILE), TILE)], row_tile, local_sem.at[2]
        ),
        pltpu.make_async_copy(
            col_hbm.at[pl.ds(pl.multiple_of(tile_row * TILE, TILE), TILE), :], col_tile, local_sem.at[3]
        ),
        pltpu.make_async_copy(col_forward_hbm, col_forward, local_sem.at[4]),
        pltpu.make_async_copy(coeff_forward_hbm, coeff_forward, local_sem.at[5]),
        pltpu.make_async_copy(row_forward_hbm, row_forward, local_sem.at[6]),
        pltpu.make_async_copy(row_inverse_hbm, row_inverse, local_sem.at[7]),
        pltpu.make_async_copy(col_inverse_hbm, col_inverse, local_sem.at[8]),
        pltpu.make_async_copy(mask_hbm, mask, local_sem.at[9]),
    ]
    for item in local:
        item.start()

    barrier = pltpu.get_barrier_semaphore()

    def greet(to_hx, to_hy):
        pl.semaphore_signal(barrier, inc=1, device_id=(to_hx, to_hy), device_id_type=MESH)

    def greet_y(i, carry):
        greet(hx, lax.rem(hy + i, n_hy))
        return carry

    def greet_z(i, carry):
        greet(x * n_z + lax.rem(z + i, n_z), hy)
        return carry

    def greet_x(i, carry):
        greet(lax.rem(x + i, n_x) * n_z + z, hy)
        return carry

    lax.fori_loop(1, n_hy, greet_y, 0)
    lax.fori_loop(1, n_z, greet_z, 0)
    lax.fori_loop(1, n_x, greet_x, 0)
    for there, to_hx in ((up, hx - 1), (down, hx + 1)):
        @pl.when(there)
        def _():
            greet(to_hx, hy)

            @pl.when(left)
            def _():
                greet(to_hx, hy - 1)

            @pl.when(right)
            def _():
                greet(to_hx, hy + 1)

    lane_group = lax.broadcasted_iota(jnp.int32, (8, COLS), 1) // BAND

    def pack(slot, value):
        for half in range(2):
            to_left = to_right = None
            for g in range(4):
                start = half * BAND + 8 * g
                rolled = value[start : start + 8, :]
                if g:
                    rolled = pltpu.roll(rolled, BAND * g, axis=1)
                if to_left is None:
                    to_left = to_right = rolled
                else:
                    to_left = jnp.where(lane_group == g, rolled, to_left)
                    to_right = jnp.where(lane_group == (g + 3) % 4, rolled, to_right)
            packed[slot, 0, 8 * half : 8 * half + 8, :] = to_left
            packed[slot, 1, 8 * half : 8 * half + 8, :] = to_right

    local[0].wait()
    accum[...] = jnp.zeros_like(accum)

    local[2].wait()
    local[3].wait()
    local[9].wait()
    active = mask[tile_row, tile_col].astype(F32)
    def distance(width, start):
        return jnp.abs(lax.broadcasted_iota(jnp.int32, (ROWS, width), 1) // ROWS + (start - place))

    far_cols = row_tile[:, pl.ds(pl.multiple_of(far_first * ROWS, 2 * ROWS), 2 * ROWS)]
    for parts_of, value, chosen in (
        (row_near, row_tile[...], distance(TILE, 0) <= NEAR),
        (row_far, far_cols, distance(2 * ROWS, far_first) > NEAR),
    ):
        high, low = split(jnp.where(chosen, value * active, 0.0))
        parts_of[...] = below(high, low) if parts_of is row_near else beside(high, low)
    for which, start in enumerate((core, 1 - core)):
        high, low = split(col_tile[pl.ds(pl.multiple_of(start * COLS, COLS), COLS), :])
        col_parts[which, 0:COLS, :] = beside(high, low)
        col_parts[which, COLS:, :] = beside(high, low)

    count = (up.astype(jnp.int32) + down.astype(jnp.int32)) * (
        1 + left.astype(jnp.int32) + right.astype(jnp.int32)
    ) + (n_hy - 1 + n_z - 1 + n_x - 1)
    pl.semaphore_wait(barrier, count)

    def prepare():
        local[1].wait()
        coeffs_pad[0 : 2 * BAND + 1, 0 : 2 * BAND + 1] = coeffs_raw[...]
        local[5].wait()
        local[6].wait()
        by_col = dot_rows(split(coeffs_pad[...]), parts(coeff_forward))
        coeff_re[...], coeff_im[...] = transform_rows(by_col, row_forward)
        for i in (4, 7, 8):
            local[i].wait()

    def remote(source_ref, target_ref, send_sem, recv_sem, to_hx, to_hy):
        return pltpu.make_async_remote_copy(
            src_ref=source_ref, dst_ref=target_ref, send_sem=send_sem, recv_sem=recv_sem,
            device_id=(to_hx, to_hy), device_id_type=MESH,
        )

    def tile_copy(slot, which, near):
        block = field.at[slot, own_rows, :]
        source_ref, target_ref = (block, block) if near else (product_send.at[slot], far.at[slot, own_far, :])
        return remote(source_ref, target_ref, tile_send.at[slot, which], tile_recv.at[slot, place], first + which, hy)

    def tile_arrival(slot, which, near):
        if near:
            block = field.at[slot, BAND + which * ROWS : BAND + (which + 1) * ROWS, :]
        else:
            block = far.at[slot, which % 2 * ROWS : (which % 2 + 1) * ROWS, :]
        return remote(block, block, tile_send.at[slot, which], tile_recv.at[slot, which], first + which, hy)

    def edge_up(slot):
        return remote(
            field.at[slot, BAND : 2 * BAND, :], field.at[slot, BAND + TILE : 2 * BAND + TILE, :],
            edge_send.at[slot, 0], edge_recv.at[slot, 1], hx - 1, hy,
        )

    def edge_down(slot):
        return remote(
            field.at[slot, TILE : TILE + BAND, :], field.at[slot, 0:BAND, :],
            edge_send.at[slot, 1], edge_recv.at[slot, 0], hx + 1, hy,
        )

    def edge_arrival(slot, which):
        rows = field.at[slot, 0:BAND, :] if which == 0 else field.at[slot, BAND + TILE : 2 * BAND + TILE, :]
        return remote(rows, rows, edge_send.at[slot, which], edge_recv.at[slot, which], hx, hy)

    def strip_copy(slot, side, which):
        to_hy = hy - 1 if side == 0 else hy + 1
        if which == 0:
            rows, target, sem, to_hx = packed.at[slot, side, 0:8, :], strips.at[slot, 1 - side, 24:32, :], 2, hx - 1
        elif which == 1:
            rows, target, sem, to_hx = packed.at[slot, side], strips.at[slot, 1 - side, 8:24, :], 1, hx
        else:
            rows, target, sem, to_hx = packed.at[slot, side, 8:16, :], strips.at[slot, 1 - side, 0:8, :], 0, hx + 1
        return remote(rows, target, strip_send.at[slot, side, which], strip_recv.at[slot, 1 - side, sem], to_hx, to_hy)

    def strip_arrival(slot, side, which):
        start, stop = ((0, 8), (8, 24), (24, 32))[which]
        rows = strips.at[slot, side, start:stop, :]
        return remote(rows, rows, strip_send.at[slot, side, which], strip_recv.at[slot, side, which], hx, hy)

    def mixed_copy(slot):
        return remote(mixed_send.at[slot], mixed_recv.at[slot], mixed_send_sem.at[slot], mixed_recv_sem.at[slot], hx, beside_core)

    def partner_copy(slot):
        return remote(
            field.at[slot, own_rows, :], partner.at[slot], partner_send.at[slot], partner_recv.at[slot], hx, beside_core
        )

    def on(conditions, action):
        if conditions:
            pl.when(functools.reduce(jnp.logical_and, conditions))(action)
        else:
            action()

    row_there = ((0, (up,)), (1, ()), (2, (down,)))
    side_there = ((0, left), (1, right))

    def tile_sends(slot, near, act):
        for distance in range(1, NEAR + 1) if near else range(GROUP - 1, NEAR, -1):
            for step in (-distance, distance):
                which = place + step
                on([which >= 0, which < GROUP], lambda which=which: act(tile_copy(slot, which, near)))

    def tile_waits(slot, near):
        for which in range(GROUP):
            distance = jnp.abs(place - which)
            chosen = [distance >= 1, distance <= NEAR] if near else [distance > NEAR]
            on(chosen, lambda which=which: tile_arrival(slot, which, near).wait_recv())

    def edge_sends(slot, act):
        on([place == 0, up], lambda: act(edge_up(slot)))
        on([place == GROUP - 1, down], lambda: act(edge_down(slot)))

    def strip_sends(slot, act):
        for which, there in (row_there[0], row_there[2], row_there[1]):
            for side, next_to in side_there:
                on([next_to, *there], lambda side=side, which=which: act(strip_copy(slot, side, which)))

    def gain(k, value):
        accum[...] += jnp.where(k == 0, 1.0, STEP) * value
        squares[pl.ds(k + ITERS - 1, 1), :] = jnp.sum(value * value, axis=0, keepdims=True)

    def begin(item):
        item.start()

    def finish(item):
        item.wait_send()

    def all_sent(slot):
        partner_copy(slot).wait_send()
        mixed_copy(slot).wait_send()
        edge_sends(slot, finish)
        tile_sends(slot, True, finish)
        strip_sends(slot, finish)
        tile_sends(slot, False, finish)

    def iteration(k, carry):
        slot = lax.rem(k, 2)
        partner_copy(slot).start()
        edge_sends(slot, begin)
        tile_sends(slot, True, begin)
        value = field[slot, own_rows, :]
        pack(slot, value)
        strip_sends(slot, begin)

        product = dot_small(beside(*split(value)), col_parts[0])
        gain(k, value)
        partner_copy(slot).wait_recv()
        product_send[slot] = product + dot_small(beside(*split(partner[slot])), col_parts[1])
        tile_sends(slot, False, begin)

        pl.when(k == 0)(prepare)

        tile_waits(slot, True)
        mixed = dot_deep(row_near[...], beside(*split(field[slot, BAND : BAND + TILE, :])))
        mixed_send[slot] = mixed
        mixed_copy(slot).start()
        total = dot_small(beside(*split(mixed)), col_parts[0])

        on([place == 0, up], lambda: edge_arrival(slot, 0).wait_recv())
        on([place == GROUP - 1, down], lambda: edge_arrival(slot, 1).wait_recv())
        tall = field[slot, pl.ds(pl.multiple_of(place * ROWS, ROWS), LONG_ROWS), :]
        for side, next_to in side_there:
            for which, there in row_there:
                on([next_to, *there], lambda side=side, which=which: strip_arrival(slot, side, which).wait_recv())
        from_left, from_right = strips[slot, 0], strips[slot, 1]
        pieces = []
        for t in range(4):
            piece_left, piece_right = from_left[8 * t : 8 * t + 8, :], from_right[8 * t : 8 * t + 8, :]
            for g in range(4):
                piece = jnp.where(
                    lane_group == g, piece_right, jnp.where(lane_group == (g + 3) % 4, piece_left, 0.0)
                )
                pieces.append(pltpu.roll(piece, COLS - BAND * g, axis=1) if g else piece)
        by_col = dot_rows(split(beside(tall, below(*pieces))), parts(col_forward))
        freq_re, freq_im = transform_rows(by_col, row_forward)
        c_re, c_im = coeff_re[...], coeff_im[...]
        high, low = split(beside(freq_re * c_re - freq_im * c_im, freq_re * c_im + freq_im * c_re))
        turned = dot(row_inverse[...], below(high, high)) + dot(row_inverse[:, 0:LONG_ROWS], low)
        cosine, sine = turned[0:ROWS], turned[ROWS:]
        back = beside(cosine[:, 0:COLS] - sine[:, COLS:], cosine[:, COLS:] + sine[:, 0:COLS])
        total = total + dot_deep(below(*split(back)), col_inverse[...])

        mixed_copy(slot).wait_recv()
        total = total + dot_small(beside(*split(mixed_recv[slot])), col_parts[1])
        pl.when(k > 0)(lambda: all_sent(1 - slot))
        keep = jnp.where(k == 0, 0.0, 1.0 - STEP)
        take = jnp.where(k == 0, 1.0, STEP)
        total = keep * value - take * total
        tile_waits(slot, False)
        field[1 - slot, own_rows, :] = total - take * dot_small(row_far[...], below(*[beside(*split(far[slot]))] * 2))
        return carry

    lax.fori_loop(0, ITERS, iteration, 0)
    gain(ITERS, field[ITERS % 2, own_rows, :])
    out_ref[...] = accum[...]
    all_sent((ITERS - 1) % 2)

    def gather(total, held, recv_sem, index, size, device):
        held[index] = total

        def copy(to, at):
            return remote(
                held.at[index], held.at[at], sum_send.at[to], recv_sem.at[at], *device(to)
            )

        def start(i, carry):
            copy(lax.rem(index + i, size), index).start()
            return carry

        def wait(i, carry):
            other = lax.rem(index + i, size)
            item = remote(held.at[other], held.at[other], sum_send.at[other], recv_sem.at[other], *device(other))
            item.wait_recv()
            copy(other, index).wait_send()
            return carry

        lax.fori_loop(1, size, start, 0)
        lax.fori_loop(1, size, wait, 0)
        return jnp.sum(held[...], axis=0)

    row, col = (lax.broadcasted_iota(jnp.int32, (ITERS, COLS), axis) for axis in (0, 1))
    sums = jnp.sum(squares[ITERS:, :], axis=1, keepdims=True)
    total = jnp.sum(jnp.where(row == col, sums, 0.0), axis=0, keepdims=True)
    total = gather(total, sum_y, sum_y_recv, hy, n_hy, lambda to: (hx, to))
    total = gather(total, sum_x.at[0:n_z], sum_x_recv.at[0], z, n_z, lambda to: (x * n_z + to, hy))
    if n_x > 1:
        total = gather(total, sum_x.at[n_z : n_z + n_x], sum_x_recv.at[1], x, n_x, lambda to: (to * n_z + z, hy))
    norm_ref[...] = jnp.sqrt(total / (ROWS * COLS * n_hx * n_hy) + TINY)


def local_step(sizes, source, coeffs, row_factor, col_factor, tile_mask):
    n_hx, n_hy = sizes
    constants = [jnp.asarray(t) for t in tables()]
    any_spec = pl.BlockSpec(memory_space=pl.ANY)
    vmem_spec = pl.BlockSpec(memory_space=pltpu.VMEM)
    dma = pltpu.SemaphoreType.DMA
    taps = 2 * BAND + 1
    scratch = [
        pltpu.VMEM((2, TILE + 2 * BAND, COLS), F32),
        pltpu.VMEM((2, ROWS, COLS), F32),
        pltpu.VMEM((2, 2 * ROWS, COLS), F32),
        pltpu.VMEM((2, ROWS, COLS), F32),
        pltpu.VMEM((2, 2, 32, COLS), F32),
        pltpu.VMEM((2, 2, 16, COLS), F32),
        pltpu.VMEM((2, ROWS, COLS), F32),
        pltpu.VMEM((2, ROWS, COLS), F32),
        pltpu.VMEM((ROWS, COLS), F32),
        pltpu.VMEM((2 * ITERS, COLS), F32),
        pltpu.SMEM((n_hx // GROUP, n_hy // 2), jnp.int32),
        pltpu.VMEM((taps, taps), F32),
        pltpu.VMEM((LONG_ROWS, COLS), F32),
        pltpu.VMEM((ROWS, TILE), F32),
        pltpu.VMEM((TILE, COLS), F32),
        pltpu.VMEM((2 * ROWS, TILE), BF16),
        pltpu.VMEM((ROWS, 4 * ROWS), BF16),
        pltpu.VMEM((2, 2 * COLS, 2 * COLS), BF16),
        pltpu.VMEM((LONG_ROWS, COLS), F32),
        pltpu.VMEM((LONG_ROWS, COLS), F32),
        *[pltpu.VMEM(c.shape, c.dtype) for c in constants],
        pltpu.VMEM((n_hy, 1, COLS), F32),
        pltpu.VMEM((n_hx, 1, COLS), F32),
        dma((10,)),
        dma((2, GROUP)), dma((2, GROUP)),
        dma((2,)), dma((2,)),
        dma((2, 2)), dma((2, 2)),
        dma((2, 2, 3)), dma((2, 2, 3)),
        dma((2,)), dma((2,)),
        dma((max(n_hy, n_hx),)), dma((n_hy,)), dma((2, n_hx)),
    ]
    result, norms = pl.pallas_call(
        functools.partial(kernel, sizes),
        out_shape=(pltpu.VMEM((ROWS, COLS), F32), pltpu.VMEM((1, COLS), F32)),
        in_specs=[any_spec] * 10,
        out_specs=(vmem_spec, vmem_spec),
        scratch_shapes=scratch,
        compiler_params=pltpu.CompilerParams(collective_id=0, has_side_effects=True),
        name="richardson",
    )(source, coeffs, row_factor, col_factor, tile_mask, *constants)
    return result, norms[0, 0:ITERS]


def solution(mesh):
    n_hx, n_hy = mesh.shape["hx"], mesh.shape["hy"]
    sizes = (n_hx, n_hy)
    in_specs = (P("hx", "hy"), P(), P("hx", None), P(None, "hy"), P())
    out_specs = (P("hx", "hy"), P())
    return jax.shard_map(
        functools.partial(local_step, sizes), mesh=mesh, in_specs=in_specs, out_specs=out_specs, check_vma=False
    )
```

```python
import functools

import jax
import jax.numpy as jnp
import ml_dtypes
import numpy as np
from jax import lax
from jax.experimental import pallas as pl
from jax.experimental.pallas import tpu as pltpu
from jax.sharding import PartitionSpec as P

TILE = 256
BAND = 32
ITERS = 8
ROWS = 64
COLS = 128
GROUP = TILE // ROWS
LONG_ROWS = ROWS + 2 * BAND
LONG_COLS = COLS + 2 * BAND
HALF = LONG_COLS // 2 + 1
NEAR = 1
STEP = 0.25
TINY = 1e-06
MESH = pl.DeviceIdType.MESH
F32 = jnp.float32
BF16 = jnp.bfloat16


def split_table(table):
    high = table.astype(np.float32).astype(ml_dtypes.bfloat16)
    low = (table - high.astype(np.float64)).astype(np.float32).astype(ml_dtypes.bfloat16)
    return high, low


def tables():
    lane = np.arange(COLS)
    freq_col = np.arange(COLS)
    kept = (freq_col < HALF).astype(np.float64)
    place = np.concatenate([lane + BAND, np.where(lane < BAND, lane + BAND + COLS, lane - (COLS - BAND))])
    used = np.concatenate([np.ones(COLS), ((lane < BAND) | (lane >= COLS - BAND)).astype(np.float64)])
    angle = 2 * np.pi * ((place[:, None] * freq_col[None, :]) % LONG_COLS) / LONG_COLS
    weight = used[:, None] * kept[None, :]
    col_forward = np.concatenate([np.cos(angle) * weight, -np.sin(angle) * weight], axis=1)
    tap = np.arange(LONG_ROWS)
    angle = 2 * np.pi * ((tap[:, None] * freq_col[None, :]) % LONG_COLS) / LONG_COLS
    weight = (tap <= 2 * BAND)[:, None] * kept[None, :]
    coeff_forward = np.concatenate([np.cos(angle) * weight, -np.sin(angle) * weight], axis=1)
    row = np.arange(LONG_ROWS)
    angle = 2 * np.pi * ((row[:, None] * row[None, :]) % LONG_ROWS) / LONG_ROWS
    order = np.concatenate([row[0::2], row[1::2]])
    halves = [angle[row[odd::2], : LONG_ROWS // 2] for odd in (0, 1)]
    row_forward = np.concatenate([f(half) for half in halves for f in (np.cos, np.sin)], axis=0)
    target = np.arange(ROWS) + 2 * BAND
    angle = 2 * np.pi * ((target[:, None] * order[None, :]) % LONG_ROWS) / LONG_ROWS
    row_inverse = np.concatenate([np.cos(angle), np.sin(angle)], axis=0)
    target = lane + 2 * BAND
    angle = 2 * np.pi * ((freq_col[:, None] * target[None, :]) % LONG_COLS) / LONG_COLS
    scale = np.where((freq_col == 0) | (freq_col == HALF - 1), 1.0, 2.0) * kept / (LONG_ROWS * LONG_COLS)
    col_inverse = np.concatenate([np.cos(angle) * scale[:, None], -np.sin(angle) * scale[:, None]], axis=0)
    high, low = split_table(row_forward)
    row_forward = np.concatenate([high, high, low, low], axis=1)
    return [
        np.concatenate(split_table(col_forward), axis=0),
        np.concatenate(split_table(coeff_forward), axis=0),
        row_forward,
        np.concatenate(split_table(row_inverse), axis=1),
        np.concatenate(split_table(col_inverse), axis=1),
    ]


def split(value):
    high = value.astype(BF16)
    return high, (value - high.astype(F32)).astype(BF16)


def dot(a, b):
    return jnp.dot(a, b, preferred_element_type=F32)


def beside(*values):
    return jnp.concatenate(values, axis=1)


def below(*values):
    return jnp.concatenate(values, axis=0)


def dot_rows(a, b):
    (a_high, a_low), (b_high, b_low) = a, b
    both = dot(below(a_high, a_low), b_high)
    count = a_high.shape[0]
    return both[0:count] + both[count:] + dot(a_high, b_low)


def dot_small(a, b):
    both = dot(a, b)
    return both[:, 0:COLS] + both[:, COLS:]


def dot_deep(a, b):
    both = dot(a, b)
    count = a.shape[0] // 2
    return both[0:count, 0:COLS] + (both[0:count, COLS:] + both[count:, 0:COLS])


def transform_rows(value, table):
    half = LONG_ROWS // 2
    top, bottom = value[0:half], value[half:]
    parts_re, parts_im = [], []
    for at, both in ((0, top + bottom), (LONG_ROWS, top - bottom)):
        high, low = split(both)
        turned = dot(table[at : at + LONG_ROWS, :], below(high, low, high, low))
        cosine, sine = turned[0:half], turned[half:]
        parts_re.append(cosine[:, 0:COLS] + sine[:, COLS:])
        parts_im.append(cosine[:, COLS:] - sine[:, 0:COLS])
    return below(*parts_re), below(*parts_im)


def around(index, size):
    return jnp.where(index >= size, index - size, index)


def parts(ref):
    half = ref.shape[0] // 2
    return ref[0:half, :], ref[half:, :]


def kernel(
    sizes,
    source_hbm, coeffs_hbm, row_hbm, col_hbm, mask_hbm,
    col_forward_hbm, coeff_forward_hbm, row_forward_hbm, row_inverse_hbm, col_inverse_hbm,
    out_ref, norm_ref,
    field, product_send, far, partner, strips, packed, mixed_send, mixed_recv, accum, squares,
    mask, coeffs_raw, coeffs_pad, row_tile, col_tile, row_near, row_far, col_parts, coeff_re, coeff_im,
    col_forward, coeff_forward, row_forward, row_inverse, col_inverse,
    sum_y, sum_x,
    local_sem, tile_send, tile_recv, partner_send, partner_recv, edge_send, edge_recv, strip_send, strip_recv,
    mixed_send_sem, mixed_recv_sem, sum_send, sum_y_recv, sum_x_recv,
):
    n_hx, n_hy = sizes
    hx, hy = lax.axis_index("hx"), lax.axis_index("hy")
    place = lax.rem(hx, GROUP)
    first = hx - place
    tile_row, tile_col = hx // GROUP, hy // 2
    core = lax.rem(hy, 2)
    up, down, left, right = hx > 0, hx < n_hx - 1, hy > 0, hy < n_hy - 1
    own_rows = pl.ds(pl.multiple_of(BAND + place * ROWS, BAND), ROWS)
    own_far = pl.ds(pl.multiple_of(lax.rem(place, 2) * ROWS, ROWS), ROWS)
    far_first = jnp.where(place < 2, 2, 0)
    beside_core = hy + 1 - 2 * core

    for slot in range(2):
        field[slot] = jnp.zeros(field.shape[1:], F32)
        far[slot] = jnp.zeros(far.shape[1:], F32)
        for side in range(2):
            strips[slot, side] = jnp.zeros((4 * 8, COLS), F32)
    coeffs_pad[...] = jnp.zeros_like(coeffs_pad)

    local = [
        pltpu.make_async_copy(source_hbm, field.at[0, own_rows, :], local_sem.at[0]),
        pltpu.make_async_copy(coeffs_hbm, coeffs_raw, local_sem.at[1]),
        pltpu.make_async_copy(
            row_hbm.at[:, pl.ds(pl.multiple_of(tile_col * TILE, TILE), TILE)], row_tile, local_sem.at[2]
        ),
        pltpu.make_async_copy(
            col_hbm.at[pl.ds(pl.multiple_of(tile_row * TILE, TILE), TILE), :], col_tile, local_sem.at[3]
        ),
        pltpu.make_async_copy(col_forward_hbm, col_forward, local_sem.at[4]),
        pltpu.make_async_copy(coeff_forward_hbm, coeff_forward, local_sem.at[5]),
        pltpu.make_async_copy(row_forward_hbm, row_forward, local_sem.at[6]),
        pltpu.make_async_copy(row_inverse_hbm, row_inverse, local_sem.at[7]),
        pltpu.make_async_copy(col_inverse_hbm, col_inverse, local_sem.at[8]),
        pltpu.make_async_copy(mask_hbm, mask, local_sem.at[9]),
    ]
    for item in local:
        item.start()

    barrier = pltpu.get_barrier_semaphore()

    def greet(to_hx, to_hy):
        pl.semaphore_signal(barrier, inc=1, device_id=(to_hx, to_hy), device_id_type=MESH)

    def greet_y(i, carry):
        greet(hx, around(hy + i, n_hy))
        return carry

    def greet_x(i, carry):
        greet(around(hx + i, n_hx), hy)
        return carry

    lax.fori_loop(1, n_hx, greet_x, 0, unroll=4)
    lax.fori_loop(1, n_hy, greet_y, 0, unroll=4)
    for there, to_hx in ((up, hx - 1), (down, hx + 1)):
        @pl.when(there)
        def _():
            @pl.when(left)
            def _():
                greet(to_hx, hy - 1)

            @pl.when(right)
            def _():
                greet(to_hx, hy + 1)

    lane_group = lax.broadcasted_iota(jnp.int32, (8, COLS), 1) // BAND

    def pack(slot, value):
        for half in range(2):
            to_left = to_right = None
            for g in range(4):
                start = half * BAND + 8 * g
                rolled = value[start : start + 8, :]
                if g:
                    rolled = pltpu.roll(rolled, BAND * g, axis=1)
                if to_left is None:
                    to_left = to_right = rolled
                else:
                    to_left = jnp.where(lane_group == g, rolled, to_left)
                    to_right = jnp.where(lane_group == (g + 3) % 4, rolled, to_right)
            packed[slot, 0, 8 * half : 8 * half + 8, :] = to_left
            packed[slot, 1, 8 * half : 8 * half + 8, :] = to_right

    local[0].wait()
    accum[...] = jnp.zeros_like(accum)

    local[2].wait()
    local[3].wait()
    local[9].wait()
    active = mask[tile_row, tile_col].astype(F32)
    def distance(width, start):
        return jnp.abs(lax.broadcasted_iota(jnp.int32, (ROWS, width), 1) // ROWS + (start - place))

    far_cols = row_tile[:, pl.ds(pl.multiple_of(far_first * ROWS, 2 * ROWS), 2 * ROWS)]
    for parts_of, value, chosen in (
        (row_near, row_tile[...], distance(TILE, 0) <= NEAR),
        (row_far, far_cols, distance(2 * ROWS, far_first) > NEAR),
    ):
        high, low = split(jnp.where(chosen, value * active, 0.0))
        parts_of[...] = below(high, low) if parts_of is row_near else beside(high, low)
    for which, start in enumerate((core, 1 - core)):
        high, low = split(col_tile[pl.ds(pl.multiple_of(start * COLS, COLS), COLS), :])
        col_parts[which, 0:COLS, :] = beside(high, low)
        col_parts[which, COLS:, :] = beside(high, low)

    count = (up.astype(jnp.int32) + down.astype(jnp.int32)) * (
        left.astype(jnp.int32) + right.astype(jnp.int32)
    ) + (n_hy - 1 + n_hx - 1)
    pl.semaphore_wait(barrier, count)

    def prepare():
        local[1].wait()
        coeffs_pad[0 : 2 * BAND + 1, 0 : 2 * BAND + 1] = coeffs_raw[...]
        local[5].wait()
        local[6].wait()
        by_col = dot_rows(split(coeffs_pad[...]), parts(coeff_forward))
        coeff_re[...], coeff_im[...] = transform_rows(by_col, row_forward)
        for i in (4, 7, 8):
            local[i].wait()

    def remote(source_ref, target_ref, send_sem, recv_sem, to_hx, to_hy):
        return pltpu.make_async_remote_copy(
            src_ref=source_ref, dst_ref=target_ref, send_sem=send_sem, recv_sem=recv_sem,
            device_id=(to_hx, to_hy), device_id_type=MESH,
        )

    def tile_copy(slot, which, near):
        block = field.at[slot, own_rows, :]
        source_ref, target_ref = (block, block) if near else (product_send.at[slot], far.at[slot, own_far, :])
        return remote(source_ref, target_ref, tile_send.at[slot, which], tile_recv.at[slot, place], first + which, hy)

    def tile_arrival(slot, which, near):
        if near:
            block = field.at[slot, BAND + which * ROWS : BAND + (which + 1) * ROWS, :]
        else:
            block = far.at[slot, which % 2 * ROWS : (which % 2 + 1) * ROWS, :]
        return remote(block, block, tile_send.at[slot, which], tile_recv.at[slot, which], first + which, hy)

    def edge_up(slot):
        return remote(
            field.at[slot, BAND : 2 * BAND, :], field.at[slot, BAND + TILE : 2 * BAND + TILE, :],
            edge_send.at[slot, 0], edge_recv.at[slot, 1], hx - 1, hy,
        )

    def edge_down(slot):
        return remote(
            field.at[slot, TILE : TILE + BAND, :], field.at[slot, 0:BAND, :],
            edge_send.at[slot, 1], edge_recv.at[slot, 0], hx + 1, hy,
        )

    def edge_arrival(slot, which):
        rows = field.at[slot, 0:BAND, :] if which == 0 else field.at[slot, BAND + TILE : 2 * BAND + TILE, :]
        return remote(rows, rows, edge_send.at[slot, which], edge_recv.at[slot, which], hx, hy)

    def strip_copy(slot, side, which):
        to_hy = hy - 1 if side == 0 else hy + 1
        if which == 0:
            rows, target, sem, to_hx = packed.at[slot, side, 0:8, :], strips.at[slot, 1 - side, 24:32, :], 2, hx - 1
        elif which == 1:
            rows, target, sem, to_hx = packed.at[slot, side], strips.at[slot, 1 - side, 8:24, :], 1, hx
        else:
            rows, target, sem, to_hx = packed.at[slot, side, 8:16, :], strips.at[slot, 1 - side, 0:8, :], 0, hx + 1
        return remote(rows, target, strip_send.at[slot, side, which], strip_recv.at[slot, 1 - side, sem], to_hx, to_hy)

    def strip_arrival(slot, side, which):
        start, stop = ((0, 8), (8, 24), (24, 32))[which]
        rows = strips.at[slot, side, start:stop, :]
        return remote(rows, rows, strip_send.at[slot, side, which], strip_recv.at[slot, side, which], hx, hy)

    def mixed_copy(slot):
        return remote(mixed_send.at[slot], mixed_recv.at[slot], mixed_send_sem.at[slot], mixed_recv_sem.at[slot], hx, beside_core)

    def partner_copy(slot):
        return remote(
            field.at[slot, own_rows, :], partner.at[slot], partner_send.at[slot], partner_recv.at[slot], hx, beside_core
        )

    def on(conditions, action):
        if conditions:
            pl.when(functools.reduce(jnp.logical_and, conditions))(action)
        else:
            action()

    row_there = ((0, (up,)), (1, ()), (2, (down,)))
    side_there = ((0, left), (1, right))

    def tile_sends(slot, near, act):
        for distance in range(1, NEAR + 1) if near else range(GROUP - 1, NEAR, -1):
            for step in (-distance, distance):
                which = place + step
                on([which >= 0, which < GROUP], lambda which=which: act(tile_copy(slot, which, near)))

    def tile_waits(slot, near):
        for which in range(GROUP):
            distance = jnp.abs(place - which)
            chosen = [distance >= 1, distance <= NEAR] if near else [distance > NEAR]
            on(chosen, lambda which=which: tile_arrival(slot, which, near).wait_recv())

    def edge_sends(slot, act):
        on([place == 0, up], lambda: act(edge_up(slot)))
        on([place == GROUP - 1, down], lambda: act(edge_down(slot)))

    def strip_sends(slot, act):
        for which, there in (row_there[0], row_there[2], row_there[1]):
            for side, next_to in side_there:
                on([next_to, *there], lambda side=side, which=which: act(strip_copy(slot, side, which)))

    def gain(k, value):
        accum[...] += jnp.where(k == 0, 1.0, STEP) * value
        squares[pl.ds(k + ITERS - 1, 1), :] = jnp.sum(value * value, axis=0, keepdims=True)

    def begin(item):
        item.start()

    def finish(item):
        item.wait_send()

    def all_sent(slot):
        partner_copy(slot).wait_send()
        mixed_copy(slot).wait_send()
        edge_sends(slot, finish)
        tile_sends(slot, True, finish)
        strip_sends(slot, finish)
        tile_sends(slot, False, finish)

    def iteration(k, carry):
        slot = lax.rem(k, 2)
        partner_copy(slot).start()
        edge_sends(slot, begin)
        tile_sends(slot, True, begin)
        value = field[slot, own_rows, :]
        pack(slot, value)
        strip_sends(slot, begin)

        product = dot_small(beside(*split(value)), col_parts[0])
        gain(k, value)
        partner_copy(slot).wait_recv()
        product_send[slot] = product + dot_small(beside(*split(partner[slot])), col_parts[1])
        tile_sends(slot, False, begin)

        pl.when(k == 0)(prepare)

        tile_waits(slot, True)
        mixed = dot_deep(row_near[...], beside(*split(field[slot, BAND : BAND + TILE, :])))
        mixed_send[slot] = mixed
        mixed_copy(slot).start()
        total = dot_small(beside(*split(mixed)), col_parts[0])

        on([place == 0, up], lambda: edge_arrival(slot, 0).wait_recv())
        on([place == GROUP - 1, down], lambda: edge_arrival(slot, 1).wait_recv())
        tall = field[slot, pl.ds(pl.multiple_of(place * ROWS, ROWS), LONG_ROWS), :]
        for side, next_to in side_there:
            for which, there in row_there:
                on([next_to, *there], lambda side=side, which=which: strip_arrival(slot, side, which).wait_recv())
        from_left, from_right = strips[slot, 0], strips[slot, 1]
        pieces = []
        for t in range(4):
            piece_left, piece_right = from_left[8 * t : 8 * t + 8, :], from_right[8 * t : 8 * t + 8, :]
            for g in range(4):
                piece = jnp.where(
                    lane_group == g, piece_right, jnp.where(lane_group == (g + 3) % 4, piece_left, 0.0)
                )
                pieces.append(pltpu.roll(piece, COLS - BAND * g, axis=1) if g else piece)
        by_col = dot_rows(split(beside(tall, below(*pieces))), parts(col_forward))
        freq_re, freq_im = transform_rows(by_col, row_forward)
        c_re, c_im = coeff_re[...], coeff_im[...]
        high, low = split(beside(freq_re * c_re - freq_im * c_im, freq_re * c_im + freq_im * c_re))
        turned = dot(row_inverse[...], below(high, high)) + dot(row_inverse[:, 0:LONG_ROWS], low)
        cosine, sine = turned[0:ROWS], turned[ROWS:]
        back = beside(cosine[:, 0:COLS] - sine[:, COLS:], cosine[:, COLS:] + sine[:, 0:COLS])
        total = total + dot_deep(below(*split(back)), col_inverse[...])

        mixed_copy(slot).wait_recv()
        total = total + dot_small(beside(*split(mixed_recv[slot])), col_parts[1])
        pl.when(k > 0)(lambda: all_sent(1 - slot))
        keep = jnp.where(k == 0, 0.0, 1.0 - STEP)
        take = jnp.where(k == 0, 1.0, STEP)
        total = keep * value - take * total
        tile_waits(slot, False)
        field[1 - slot, own_rows, :] = total - take * dot_small(row_far[...], below(*[beside(*split(far[slot]))] * 2))
        return carry

    lax.fori_loop(0, ITERS, iteration, 0)
    gain(ITERS, field[ITERS % 2, own_rows, :])
    out_ref[...] = accum[...]
    all_sent((ITERS - 1) % 2)

    def gather(total, held, recv_sem, index, size, device):
        held[index] = total

        def copy(to, at):
            return remote(
                held.at[index], held.at[at], sum_send.at[to], recv_sem.at[at], *device(to)
            )

        def start(i, carry):
            copy(around(index + i, size), index).start()
            return carry

        def wait(i, carry):
            other = around(index + i, size)
            item = remote(held.at[other], held.at[other], sum_send.at[other], recv_sem.at[other], *device(other))
            item.wait_recv()
            copy(other, index).wait_send()
            return carry

        lax.fori_loop(1, size, start, 0, unroll=4)
        lax.fori_loop(1, size, wait, 0)
        return jnp.sum(held[...], axis=0)

    row, col = (lax.broadcasted_iota(jnp.int32, (ITERS, COLS), axis) for axis in (0, 1))
    sums = jnp.sum(squares[ITERS:, :], axis=1, keepdims=True)
    total = jnp.sum(jnp.where(row == col, sums, 0.0), axis=0, keepdims=True)
    total = gather(total, sum_y, sum_y_recv, hy, n_hy, lambda to: (hx, to))
    total = gather(total, sum_x, sum_x_recv, hx, n_hx, lambda to: (to, hy))
    norm_ref[...] = jnp.sqrt(total / (ROWS * COLS * n_hx * n_hy) + TINY)


def local_step(sizes, source, coeffs, row_factor, col_factor, tile_mask):
    n_hx, n_hy = sizes
    constants = [jnp.asarray(t) for t in tables()]
    any_spec = pl.BlockSpec(memory_space=pl.ANY)
    vmem_spec = pl.BlockSpec(memory_space=pltpu.VMEM)
    dma = pltpu.SemaphoreType.DMA
    taps = 2 * BAND + 1
    scratch = [
        pltpu.VMEM((2, TILE + 2 * BAND, COLS), F32),
        pltpu.VMEM((2, ROWS, COLS), F32),
        pltpu.VMEM((2, 2 * ROWS, COLS), F32),
        pltpu.VMEM((2, ROWS, COLS), F32),
        pltpu.VMEM((2, 2, 32, COLS), F32),
        pltpu.VMEM((2, 2, 16, COLS), F32),
        pltpu.VMEM((2, ROWS, COLS), F32),
        pltpu.VMEM((2, ROWS, COLS), F32),
        pltpu.VMEM((ROWS, COLS), F32),
        pltpu.VMEM((2 * ITERS, COLS), F32),
        pltpu.SMEM((n_hx // GROUP, n_hy // 2), jnp.int32),
        pltpu.VMEM((taps, taps), F32),
        pltpu.VMEM((LONG_ROWS, COLS), F32),
        pltpu.VMEM((ROWS, TILE), F32),
        pltpu.VMEM((TILE, COLS), F32),
        pltpu.VMEM((2 * ROWS, TILE), BF16),
        pltpu.VMEM((ROWS, 4 * ROWS), BF16),
        pltpu.VMEM((2, 2 * COLS, 2 * COLS), BF16),
        pltpu.VMEM((LONG_ROWS, COLS), F32),
        pltpu.VMEM((LONG_ROWS, COLS), F32),
        *[pltpu.VMEM(c.shape, c.dtype) for c in constants],
        pltpu.VMEM((n_hy, 1, COLS), F32),
        pltpu.VMEM((n_hx, 1, COLS), F32),
        dma((10,)),
        dma((2, GROUP)), dma((2, GROUP)),
        dma((2,)), dma((2,)),
        dma((2, 2)), dma((2, 2)),
        dma((2, 2, 3)), dma((2, 2, 3)),
        dma((2,)), dma((2,)),
        dma((max(n_hy, n_hx),)), dma((n_hy,)), dma((n_hx,)),
    ]
    result, norms = pl.pallas_call(
        functools.partial(kernel, sizes),
        out_shape=(pltpu.VMEM((ROWS, COLS), F32), pltpu.VMEM((1, COLS), F32)),
        in_specs=[any_spec] * 10,
        out_specs=(vmem_spec, vmem_spec),
        scratch_shapes=scratch,
        compiler_params=pltpu.CompilerParams(collective_id=0, has_side_effects=True),
        name="richardson",
    )(source, coeffs, row_factor, col_factor, tile_mask, *constants)
    return result, norms[0, 0:ITERS]


def solution(mesh):
    n_hx, n_hy = mesh.shape["hx"], mesh.shape["hy"]
    sizes = (n_hx, n_hy)
    in_specs = (P("hx", "hy"), P(), P("hx", None), P(None, "hy"), P())
    out_specs = (P("hx", "hy"), P())
    return jax.shard_map(
        functools.partial(local_step, sizes), mesh=mesh, in_specs=in_specs, out_specs=out_specs, check_vma=False
    )
```

```python
import functools

import jax
import jax.numpy as jnp
import ml_dtypes
import numpy as np
from jax import lax
from jax.experimental import pallas as pl
from jax.experimental.pallas import tpu as pltpu
from jax.sharding import PartitionSpec as P

TILE = 256
BAND = 32
ITERS = 8
ROWS = 64
COLS = 128
GROUP = TILE // ROWS
LONG_ROWS = ROWS + 2 * BAND
LONG_COLS = COLS + 2 * BAND
HALF = LONG_COLS // 2 + 1
NEAR = 1
STEP = 0.25
TINY = 1e-06
MESH = pl.DeviceIdType.MESH
F32 = jnp.float32
BF16 = jnp.bfloat16


def split_table(table):
    high = table.astype(np.float32).astype(ml_dtypes.bfloat16)
    low = (table - high.astype(np.float64)).astype(np.float32).astype(ml_dtypes.bfloat16)
    return high, low


def tables():
    lane = np.arange(COLS)
    freq_col = np.arange(COLS)
    kept = (freq_col < HALF).astype(np.float64)
    place = np.concatenate([lane + BAND, np.where(lane < BAND, lane + BAND + COLS, lane - (COLS - BAND))])
    used = np.concatenate([np.ones(COLS), ((lane < BAND) | (lane >= COLS - BAND)).astype(np.float64)])
    angle = 2 * np.pi * ((place[:, None] * freq_col[None, :]) % LONG_COLS) / LONG_COLS
    weight = used[:, None] * kept[None, :]
    col_forward = np.concatenate([np.cos(angle) * weight, -np.sin(angle) * weight], axis=1)
    tap = np.arange(LONG_ROWS)
    angle = 2 * np.pi * ((tap[:, None] * freq_col[None, :]) % LONG_COLS) / LONG_COLS
    weight = (tap <= 2 * BAND)[:, None] * kept[None, :]
    coeff_forward = np.concatenate([np.cos(angle) * weight, -np.sin(angle) * weight], axis=1)
    row = np.arange(LONG_ROWS)
    angle = 2 * np.pi * ((row[:, None] * row[None, :]) % LONG_ROWS) / LONG_ROWS
    order = np.concatenate([row[0::2], row[1::2]])
    halves = [angle[row[odd::2], : LONG_ROWS // 2] for odd in (0, 1)]
    row_forward = np.concatenate([f(half) for half in halves for f in (np.cos, np.sin)], axis=0)
    target = np.arange(ROWS) + 2 * BAND
    angle = 2 * np.pi * ((target[:, None] * order[None, :]) % LONG_ROWS) / LONG_ROWS
    row_inverse = np.concatenate([np.cos(angle), np.sin(angle)], axis=0)
    target = lane + 2 * BAND
    angle = 2 * np.pi * ((freq_col[:, None] * target[None, :]) % LONG_COLS) / LONG_COLS
    scale = np.where((freq_col == 0) | (freq_col == HALF - 1), 1.0, 2.0) * kept / (LONG_ROWS * LONG_COLS)
    col_inverse = np.concatenate([np.cos(angle) * scale[:, None], -np.sin(angle) * scale[:, None]], axis=0)
    high, low = split_table(row_forward)
    row_forward = np.concatenate([high, high, low, low], axis=1)
    return [
        np.concatenate(split_table(col_forward), axis=0),
        np.concatenate(split_table(coeff_forward), axis=0),
        row_forward,
        np.concatenate(split_table(row_inverse), axis=1),
        np.concatenate(split_table(col_inverse), axis=1),
    ]


def split(value):
    high = value.astype(BF16)
    return high, (value - high.astype(F32)).astype(BF16)


def dot(a, b):
    return jnp.dot(a, b, preferred_element_type=F32)


def beside(*values):
    return jnp.concatenate(values, axis=1)


def below(*values):
    return jnp.concatenate(values, axis=0)


def dot_rows(a, b):
    (a_high, a_low), (b_high, b_low) = a, b
    both = dot(below(a_high, a_low), b_high)
    count = a_high.shape[0]
    return both[0:count] + both[count:] + dot(a_high, b_low)


def dot_small(a, b):
    both = dot(a, b)
    return both[:, 0:COLS] + both[:, COLS:]


def dot_deep(a, b):
    both = dot(a, b)
    count = a.shape[0] // 2
    return both[0:count, 0:COLS] + (both[0:count, COLS:] + both[count:, 0:COLS])


def transform_rows(value, table):
    half = LONG_ROWS // 2
    top, bottom = value[0:half], value[half:]
    parts_re, parts_im = [], []
    for at, both in ((0, top + bottom), (LONG_ROWS, top - bottom)):
        high, low = split(both)
        turned = dot(table[at : at + LONG_ROWS, :], below(high, low, high, low))
        cosine, sine = turned[0:half], turned[half:]
        parts_re.append(cosine[:, 0:COLS] + sine[:, COLS:])
        parts_im.append(cosine[:, COLS:] - sine[:, 0:COLS])
    return below(*parts_re), below(*parts_im)


def around(index, size):
    return jnp.where(index >= size, index - size, index)


def parts(ref):
    half = ref.shape[0] // 2
    return ref[0:half, :], ref[half:, :]


def kernel(
    sizes,
    source_hbm, coeffs_hbm, row_hbm, col_hbm, mask_hbm,
    col_forward_hbm, coeff_forward_hbm, row_forward_hbm, row_inverse_hbm, col_inverse_hbm,
    out_ref, norm_ref,
    field, product_send, far, partner, strips, packed, mixed_send, mixed_recv, accum, squares,
    mask, coeffs_raw, coeffs_pad, row_tile, col_tile, row_near, row_far, col_parts, coeff_re, coeff_im,
    col_forward, coeff_forward, row_forward, row_inverse, col_inverse,
    sum_y, sum_x,
    local_sem, tile_send, tile_recv, partner_send, partner_recv, edge_send, edge_recv, strip_send, strip_recv,
    mixed_send_sem, mixed_recv_sem, sum_send, sum_y_recv, sum_x_recv,
):
    n_hx, n_hy = sizes
    hx, hy = lax.axis_index("hx"), lax.axis_index("hy")
    place = lax.rem(hx, GROUP)
    first = hx - place
    tile_row, tile_col = hx // GROUP, hy // 2
    core = lax.rem(hy, 2)
    up, down, left, right = hx > 0, hx < n_hx - 1, hy > 0, hy < n_hy - 1
    own_rows = pl.ds(pl.multiple_of(BAND + place * ROWS, BAND), ROWS)
    own_far = pl.ds(pl.multiple_of(lax.rem(place, 2) * ROWS, ROWS), ROWS)
    far_first = jnp.where(place < 2, 2, 0)
    beside_core = hy + 1 - 2 * core

    for slot in range(2):
        field[slot] = jnp.zeros(field.shape[1:], F32)
        far[slot] = jnp.zeros(far.shape[1:], F32)
        for side in range(2):
            strips[slot, side] = jnp.zeros((4 * 8, COLS), F32)
    coeffs_pad[...] = jnp.zeros_like(coeffs_pad)

    local = [
        pltpu.make_async_copy(source_hbm, field.at[0, own_rows, :], local_sem.at[0]),
        pltpu.make_async_copy(coeffs_hbm, coeffs_raw, local_sem.at[1]),
        pltpu.make_async_copy(
            row_hbm.at[:, pl.ds(pl.multiple_of(tile_col * TILE, TILE), TILE)], row_tile, local_sem.at[2]
        ),
        pltpu.make_async_copy(
            col_hbm.at[pl.ds(pl.multiple_of(tile_row * TILE, TILE), TILE), :], col_tile, local_sem.at[3]
        ),
        pltpu.make_async_copy(col_forward_hbm, col_forward, local_sem.at[4]),
        pltpu.make_async_copy(coeff_forward_hbm, coeff_forward, local_sem.at[5]),
        pltpu.make_async_copy(row_forward_hbm, row_forward, local_sem.at[6]),
        pltpu.make_async_copy(row_inverse_hbm, row_inverse, local_sem.at[7]),
        pltpu.make_async_copy(col_inverse_hbm, col_inverse, local_sem.at[8]),
        pltpu.make_async_copy(mask_hbm, mask, local_sem.at[9]),
    ]
    for item in local:
        item.start()

    barrier = pltpu.get_barrier_semaphore()

    def greet(to_hx, to_hy):
        pl.semaphore_signal(barrier, inc=1, device_id=(to_hx, to_hy), device_id_type=MESH)

    def greet_y(i, carry):
        greet(hx, around(hy + i, n_hy))
        return carry

    def greet_x(i, carry):
        greet(around(hx + i, n_hx), hy)
        return carry

    lax.fori_loop(1, n_hx, greet_x, 0, unroll=4)
    lax.fori_loop(1, n_hy, greet_y, 0, unroll=4)
    for there, to_hx in ((up, hx - 1), (down, hx + 1)):
        @pl.when(there)
        def _():
            @pl.when(left)
            def _():
                greet(to_hx, hy - 1)

            @pl.when(right)
            def _():
                greet(to_hx, hy + 1)

    lane_group = lax.broadcasted_iota(jnp.int32, (8, COLS), 1) // BAND

    def pack(slot, value):
        for half in range(2):
            to_left = to_right = None
            for g in range(4):
                start = half * BAND + 8 * g
                rolled = value[start : start + 8, :]
                if g:
                    rolled = pltpu.roll(rolled, BAND * g, axis=1)
                if to_left is None:
                    to_left = to_right = rolled
                else:
                    to_left = jnp.where(lane_group == g, rolled, to_left)
                    to_right = jnp.where(lane_group == (g + 3) % 4, rolled, to_right)
            packed[slot, 0, 8 * half : 8 * half + 8, :] = to_left
            packed[slot, 1, 8 * half : 8 * half + 8, :] = to_right

    local[0].wait()
    accum[...] = jnp.zeros_like(accum)

    local[2].wait()
    local[3].wait()
    local[9].wait()
    active = mask[tile_row, tile_col].astype(F32)
    def distance(width, start):
        return jnp.abs(lax.broadcasted_iota(jnp.int32, (ROWS, width), 1) // ROWS + (start - place))

    far_cols = row_tile[:, pl.ds(pl.multiple_of(far_first * ROWS, 2 * ROWS), 2 * ROWS)]
    for parts_of, value, chosen in (
        (row_near, row_tile[...], distance(TILE, 0) <= NEAR),
        (row_far, far_cols, distance(2 * ROWS, far_first) > NEAR),
    ):
        high, low = split(jnp.where(chosen, value * active, 0.0))
        parts_of[...] = below(high, low) if parts_of is row_near else beside(high, low)
    for which, start in enumerate((core, 1 - core)):
        high, low = split(col_tile[pl.ds(pl.multiple_of(start * COLS, COLS), COLS), :])
        col_parts[which, 0:COLS, :] = beside(high, low)
        col_parts[which, COLS:, :] = beside(high, low)

    count = (up.astype(jnp.int32) + down.astype(jnp.int32)) * (
        left.astype(jnp.int32) + right.astype(jnp.int32)
    ) + (n_hy - 1 + n_hx - 1)
    pl.semaphore_wait(barrier, count)

    def prepare():
        local[1].wait()
        coeffs_pad[0 : 2 * BAND + 1, 0 : 2 * BAND + 1] = coeffs_raw[...]
        local[5].wait()
        local[6].wait()
        by_col = dot_rows(split(coeffs_pad[...]), parts(coeff_forward))
        coeff_re[...], coeff_im[...] = transform_rows(by_col, row_forward)
        for i in (4, 7, 8):
            local[i].wait()

    def remote(source_ref, target_ref, send_sem, recv_sem, to_hx, to_hy):
        return pltpu.make_async_remote_copy(
            src_ref=source_ref, dst_ref=target_ref, send_sem=send_sem, recv_sem=recv_sem,
            device_id=(to_hx, to_hy), device_id_type=MESH,
        )

    def tile_copy(slot, which, near):
        block = field.at[slot, own_rows, :]
        source_ref, target_ref = (block, block) if near else (product_send.at[slot], far.at[slot, own_far, :])
        return remote(source_ref, target_ref, tile_send.at[slot, which], tile_recv.at[slot, place], first + which, hy)

    def tile_arrival(slot, which, near):
        if near:
            block = field.at[slot, BAND + which * ROWS : BAND + (which + 1) * ROWS, :]
        else:
            block = far.at[slot, which % 2 * ROWS : (which % 2 + 1) * ROWS, :]
        return remote(block, block, tile_send.at[slot, which], tile_recv.at[slot, which], first + which, hy)

    def edge_up(slot):
        return remote(
            field.at[slot, BAND : 2 * BAND, :], field.at[slot, BAND + TILE : 2 * BAND + TILE, :],
            edge_send.at[slot, 0], edge_recv.at[slot, 1], hx - 1, hy,
        )

    def edge_down(slot):
        return remote(
            field.at[slot, TILE : TILE + BAND, :], field.at[slot, 0:BAND, :],
            edge_send.at[slot, 1], edge_recv.at[slot, 0], hx + 1, hy,
        )

    def edge_arrival(slot, which):
        rows = field.at[slot, 0:BAND, :] if which == 0 else field.at[slot, BAND + TILE : 2 * BAND + TILE, :]
        return remote(rows, rows, edge_send.at[slot, which], edge_recv.at[slot, which], hx, hy)

    def strip_copy(slot, side, which):
        to_hy = hy - 1 if side == 0 else hy + 1
        if which == 0:
            rows, target, sem, to_hx = packed.at[slot, side, 0:8, :], strips.at[slot, 1 - side, 24:32, :], 2, hx - 1
        elif which == 1:
            rows, target, sem, to_hx = packed.at[slot, side], strips.at[slot, 1 - side, 8:24, :], 1, hx
        else:
            rows, target, sem, to_hx = packed.at[slot, side, 8:16, :], strips.at[slot, 1 - side, 0:8, :], 0, hx + 1
        return remote(rows, target, strip_send.at[slot, side, which], strip_recv.at[slot, 1 - side, sem], to_hx, to_hy)

    def strip_arrival(slot, side, which):
        start, stop = ((0, 8), (8, 24), (24, 32))[which]
        rows = strips.at[slot, side, start:stop, :]
        return remote(rows, rows, strip_send.at[slot, side, which], strip_recv.at[slot, side, which], hx, hy)

    def mixed_copy(slot):
        return remote(mixed_send.at[slot], mixed_recv.at[slot], mixed_send_sem.at[slot], mixed_recv_sem.at[slot], hx, beside_core)

    def partner_copy(slot):
        return remote(
            field.at[slot, own_rows, :], partner.at[slot], partner_send.at[slot], partner_recv.at[slot], hx, beside_core
        )

    def on(conditions, action):
        if conditions:
            pl.when(functools.reduce(jnp.logical_and, conditions))(action)
        else:
            action()

    row_there = ((0, (up,)), (1, ()), (2, (down,)))
    side_there = ((0, left), (1, right))

    def tile_sends(slot, near, act):
        for distance in range(1, NEAR + 1) if near else range(GROUP - 1, NEAR, -1):
            for step in (-distance, distance):
                which = place + step
                on([which >= 0, which < GROUP], lambda which=which: act(tile_copy(slot, which, near)))

    def tile_waits(slot, near):
        for which in range(GROUP):
            distance = jnp.abs(place - which)
            chosen = [distance >= 1, distance <= NEAR] if near else [distance > NEAR]
            on(chosen, lambda which=which: tile_arrival(slot, which, near).wait_recv())

    def edge_sends(slot, act):
        on([place == 0, up], lambda: act(edge_up(slot)))
        on([place == GROUP - 1, down], lambda: act(edge_down(slot)))

    def strip_sends(slot, act):
        for which, there in (row_there[0], row_there[2], row_there[1]):
            for side, next_to in side_there:
                on([next_to, *there], lambda side=side, which=which: act(strip_copy(slot, side, which)))

    def gain(k, value):
        accum[...] += jnp.where(k == 0, 1.0, STEP) * value
        squares[pl.ds(k + ITERS - 1, 1), :] = jnp.sum(value * value, axis=0, keepdims=True)

    def begin(item):
        item.start()

    def finish(item):
        item.wait_send()

    def all_sent(slot):
        partner_copy(slot).wait_send()
        mixed_copy(slot).wait_send()
        edge_sends(slot, finish)
        tile_sends(slot, True, finish)
        strip_sends(slot, finish)
        tile_sends(slot, False, finish)

    def iteration(k, carry):
        slot = lax.rem(k, 2)
        partner_copy(slot).start()
        edge_sends(slot, begin)
        tile_sends(slot, True, begin)
        value = field[slot, own_rows, :]
        pack(slot, value)
        strip_sends(slot, begin)

        product = dot_small(beside(*split(value)), col_parts[0])
        gain(k, value)
        partner_copy(slot).wait_recv()
        product_send[slot] = product + dot_small(beside(*split(partner[slot])), col_parts[1])
        tile_sends(slot, False, begin)

        pl.when(k == 0)(prepare)

        tile_waits(slot, True)
        near_high, near_low = parts(row_near)
        high, low = split(field[slot, BAND : BAND + TILE, :])
        mixed = dot(near_high, high) + dot(near_high, low) + dot(near_low, high)
        mixed_send[slot] = mixed
        mixed_copy(slot).start()
        total = dot_small(beside(*split(mixed)), col_parts[0])

        on([place == 0, up], lambda: edge_arrival(slot, 0).wait_recv())
        on([place == GROUP - 1, down], lambda: edge_arrival(slot, 1).wait_recv())
        tall = field[slot, pl.ds(pl.multiple_of(place * ROWS, ROWS), LONG_ROWS), :]
        for side, next_to in side_there:
            for which, there in row_there:
                on([next_to, *there], lambda side=side, which=which: strip_arrival(slot, side, which).wait_recv())
        from_left, from_right = strips[slot, 0], strips[slot, 1]
        pieces = []
        for t in range(4):
            piece_left, piece_right = from_left[8 * t : 8 * t + 8, :], from_right[8 * t : 8 * t + 8, :]
            for g in range(4):
                piece = jnp.where(
                    lane_group == g, piece_right, jnp.where(lane_group == (g + 3) % 4, piece_left, 0.0)
                )
                pieces.append(pltpu.roll(piece, COLS - BAND * g, axis=1) if g else piece)
        by_col = dot_rows(split(beside(tall, below(*pieces))), parts(col_forward))
        freq_re, freq_im = transform_rows(by_col, row_forward)
        c_re, c_im = coeff_re[...], coeff_im[...]
        high, low = split(beside(freq_re * c_re - freq_im * c_im, freq_re * c_im + freq_im * c_re))
        turned = dot(row_inverse[...], below(high, high)) + dot(row_inverse[:, 0:LONG_ROWS], low)
        cosine, sine = turned[0:ROWS], turned[ROWS:]
        back = beside(cosine[:, 0:COLS] - sine[:, COLS:], cosine[:, COLS:] + sine[:, 0:COLS])
        total = total + dot_deep(below(*split(back)), col_inverse[...])

        mixed_copy(slot).wait_recv()
        total = total + dot_small(beside(*split(mixed_recv[slot])), col_parts[1])
        pl.when(k > 0)(lambda: all_sent(1 - slot))
        keep = jnp.where(k == 0, 0.0, 1.0 - STEP)
        take = jnp.where(k == 0, 1.0, STEP)
        total = keep * value - take * total
        tile_waits(slot, False)
        field[1 - slot, own_rows, :] = total - take * dot_small(row_far[...], below(*[beside(*split(far[slot]))] * 2))
        return carry

    lax.fori_loop(0, ITERS, iteration, 0)
    gain(ITERS, field[ITERS % 2, own_rows, :])
    out_ref[...] = accum[...]
    all_sent((ITERS - 1) % 2)

    def gather(total, held, recv_sem, index, size, device):
        held[index] = total

        def copy(to, at):
            return remote(
                held.at[index], held.at[at], sum_send.at[to], recv_sem.at[at], *device(to)
            )

        def start(i, carry):
            copy(around(index + i, size), index).start()
            return carry

        def wait(i, carry):
            other = around(index + i, size)
            item = remote(held.at[other], held.at[other], sum_send.at[other], recv_sem.at[other], *device(other))
            item.wait_recv()
            copy(other, index).wait_send()
            return carry

        lax.fori_loop(1, size, start, 0, unroll=4)
        lax.fori_loop(1, size, wait, 0)
        return jnp.sum(held[...], axis=0)

    row, col = (lax.broadcasted_iota(jnp.int32, (ITERS, COLS), axis) for axis in (0, 1))
    sums = jnp.sum(squares[ITERS:, :], axis=1, keepdims=True)
    total = jnp.sum(jnp.where(row == col, sums, 0.0), axis=0, keepdims=True)
    total = gather(total, sum_y, sum_y_recv, hy, n_hy, lambda to: (hx, to))
    total = gather(total, sum_x, sum_x_recv, hx, n_hx, lambda to: (to, hy))
    norm_ref[...] = jnp.sqrt(total / (ROWS * COLS * n_hx * n_hy) + TINY)


def local_step(sizes, source, coeffs, row_factor, col_factor, tile_mask):
    n_hx, n_hy = sizes
    constants = [jnp.asarray(t) for t in tables()]
    any_spec = pl.BlockSpec(memory_space=pl.ANY)
    vmem_spec = pl.BlockSpec(memory_space=pltpu.VMEM)
    dma = pltpu.SemaphoreType.DMA
    taps = 2 * BAND + 1
    scratch = [
        pltpu.VMEM((2, TILE + 2 * BAND, COLS), F32),
        pltpu.VMEM((2, ROWS, COLS), F32),
        pltpu.VMEM((2, 2 * ROWS, COLS), F32),
        pltpu.VMEM((2, ROWS, COLS), F32),
        pltpu.VMEM((2, 2, 32, COLS), F32),
        pltpu.VMEM((2, 2, 16, COLS), F32),
        pltpu.VMEM((2, ROWS, COLS), F32),
        pltpu.VMEM((2, ROWS, COLS), F32),
        pltpu.VMEM((ROWS, COLS), F32),
        pltpu.VMEM((2 * ITERS, COLS), F32),
        pltpu.SMEM((n_hx // GROUP, n_hy // 2), jnp.int32),
        pltpu.VMEM((taps, taps), F32),
        pltpu.VMEM((LONG_ROWS, COLS), F32),
        pltpu.VMEM((ROWS, TILE), F32),
        pltpu.VMEM((TILE, COLS), F32),
        pltpu.VMEM((2 * ROWS, TILE), BF16),
        pltpu.VMEM((ROWS, 4 * ROWS), BF16),
        pltpu.VMEM((2, 2 * COLS, 2 * COLS), BF16),
        pltpu.VMEM((LONG_ROWS, COLS), F32),
        pltpu.VMEM((LONG_ROWS, COLS), F32),
        *[pltpu.VMEM(c.shape, c.dtype) for c in constants],
        pltpu.VMEM((n_hy, 1, COLS), F32),
        pltpu.VMEM((n_hx, 1, COLS), F32),
        dma((10,)),
        dma((2, GROUP)), dma((2, GROUP)),
        dma((2,)), dma((2,)),
        dma((2, 2)), dma((2, 2)),
        dma((2, 2, 3)), dma((2, 2, 3)),
        dma((2,)), dma((2,)),
        dma((max(n_hy, n_hx),)), dma((n_hy,)), dma((n_hx,)),
    ]
    result, norms = pl.pallas_call(
        functools.partial(kernel, sizes),
        out_shape=(pltpu.VMEM((ROWS, COLS), F32), pltpu.VMEM((1, COLS), F32)),
        in_specs=[any_spec] * 10,
        out_specs=(vmem_spec, vmem_spec),
        scratch_shapes=scratch,
        compiler_params=pltpu.CompilerParams(collective_id=0, has_side_effects=True),
        name="richardson",
    )(source, coeffs, row_factor, col_factor, tile_mask, *constants)
    return result, norms[0, 0:ITERS]


def solution(mesh):
    n_hx, n_hy = mesh.shape["hx"], mesh.shape["hy"]
    sizes = (n_hx, n_hy)
    in_specs = (P("hx", "hy"), P(), P("hx", None), P(None, "hy"), P())
    out_specs = (P("hx", "hy"), P())
    return jax.shard_map(
        functools.partial(local_step, sizes), mesh=mesh, in_specs=in_specs, out_specs=out_specs, check_vma=False
    )
```
